1024 devices in a mesh: gx: 8 (over z_hi, x), gy: 16 (over z_lo), gz: 8 (over y, core).
Axes of the slice: x: 4, y: 4, z: 32 (z_hi: 2, z_lo: 16; z = z_hi * 16 + z_lo), core: 2. Of those that a mesh axis runs over, the one named last changes fastest.
Arguments:
- right_side: float32 [64, 256, 1024], P('gx', 'gy', 'gz'), may hold values from -6 to 6
- coefficient: float32 [64, 256, 1024], P('gx', 'gy', 'gz'), may hold values from 0.25 to 4
Outputs:
- solution: float32 [64, 256, 1024], P('gx', 'gy', 'gz')
- residual: float32 [64, 256, 1024], P('gx', 'gy', 'gz')
The draws below stay inside these ranges and needn't reach their ends.
All inputs are finite; a program needn't handle non-finite values.
Results may differ from the reference program's by a relative error of at most 0.0003.
Values sent between devices are 32-bit elements; how exact they have to be, the bound alone decides.
A program may use at most 32 MiB of HBM per device.

```python
import math
import jax
import jax.numpy as jnp

LEVELS = 3
DEGREE = 4
NX = 64
NY = 256
NZ = 1024


def draw_right_side(key, part):
    return jnp.clip(jax.random.normal(key, (NX, NY, NZ), jnp.float32), -6.0, 6.0)


def block_levels(rng, shape, shards, smallest, top_value):
    def one(dim, parts):
        heights = jax.random.uniform(jax.random.fold_in(jax.random.fold_in(rng, 6), dim), (parts,), jnp.float32, smallest / len(shards), top_value / len(shards))
        return jnp.repeat(jnp.exp(heights), shape[dim] // parts).reshape((-1,) + (1,) * (len(shape) - dim - 1))

    factor_of = one(*shards[0])
    for cut in shards[1:]:
        factor_of = factor_of * one(*cut)
    return factor_of


def setup_inputs(seed: int = 0) -> dict:
    key_list = jax.random.split(jax.random.key(seed), 3)
    right_side = draw_right_side(jax.random.fold_in(key_list[2], 71), 0)
    coefficient = jnp.clip(jnp.exp(math.log(4.0) - 2.7725887 * jax.random.uniform(key_list[1], (NX, NY, NZ), jnp.float32) ** block_levels(key_list[1], (NX, NY, NZ), ((0, 8), (1, 16), (2, 8)), -0.2, 0.2)), 0.25, 4.0)
    return {"right_side": right_side, "coefficient": coefficient}


cheb_low = 0.3
cheb_high = 2.0


def face_terms(padded):
    face_x = 0.5 * (padded[1:, 1:-1, 1:-1] + padded[:-1, 1:-1, 1:-1])
    face_y = 0.5 * (padded[1:-1, 1:, 1:-1] + padded[1:-1, :-1, 1:-1])
    face_z = 0.5 * (padded[1:-1, 1:-1, 1:] + padded[1:-1, 1:-1, :-1])
    diagonal = face_x[1:] + face_x[:-1] + face_y[:, 1:] + face_y[:, :-1] + face_z[:, :, 1:] + face_z[:, :, :-1]
    return face_x, face_y, face_z, diagonal


def apply_padded(padded, face_set, factor):
    face_x, face_y, face_z, diagonal = face_set
    flux_x = face_x * (padded[1:, 1:-1, 1:-1] - padded[:-1, 1:-1, 1:-1])
    flux_y = face_y * (padded[1:-1, 1:, 1:-1] - padded[1:-1, :-1, 1:-1])
    flux_z = face_z * (padded[1:-1, 1:-1, 1:] - padded[1:-1, 1:-1, :-1])
    result = (flux_x[:-1] - flux_x[1:]) + (flux_y[:, :-1] - flux_y[:, 1:]) + (flux_z[:, :, :-1] - flux_z[:, :, 1:])
    return factor * result


def zero_pad(values):
    return jnp.pad(values, 1)


def restrict(values):
    size_x, size_y, size_z = values.shape
    blocks = values.reshape(size_x // 2, 2, size_y // 2, 2, size_z // 2, 2)
    return jnp.mean(blocks, axis=(1, 3, 5))


def prolong(values):
    size_x, size_y, size_z = values.shape
    spread = jnp.broadcast_to(values[:, None, :, None, :, None], (size_x, 2, size_y, 2, size_z, 2))
    return spread.reshape(2 * size_x, 2 * size_y, 2 * size_z)


def smooth(right, initial, face_set, factor, padder):
    diagonal = face_set[3]
    centre = 0.5 * (cheb_high + cheb_low)
    half_width = 0.5 * (cheb_high - cheb_low)
    sigma_val = centre / half_width
    rho_now = 1.0 / sigma_val
    if initial is None:
        iterate = jnp.zeros_like(right)
        leftover = right
    else:
        iterate = initial
        leftover = right - apply_padded(padder(initial), face_set, factor)
    update = leftover / (factor * diagonal) / centre
    iterate = iterate + update
    for sweep_no in range(DEGREE - 1):
        leftover = right - apply_padded(padder(iterate), face_set, factor)
        rho_next = 1.0 / (2.0 * sigma_val - rho_now)
        update = rho_next * rho_now * update + (2.0 * rho_next / half_width) * (leftover / (factor * diagonal))
        iterate = iterate + update
        rho_now = rho_next
    return iterate


def reference(right_side, coefficient):
    rights = [right_side]
    coarse_coef = coefficient
    face_sets = []
    iterates = []
    for level_no in range(LEVELS):
        factor = 0.25 ** level_no
        face_set = face_terms(zero_pad(coarse_coef))
        face_sets.append(face_set)
        current = smooth(rights[-1], None, face_set, factor, zero_pad)
        iterates.append(current)
        if level_no < LEVELS - 1:
            leftover = rights[-1] - apply_padded(zero_pad(current), face_set, factor)
            rights.append(restrict(leftover))
            coarse_coef = restrict(coarse_coef)
    for level_no in range(LEVELS - 2, -1, -1):
        iterates[level_no] = smooth(rights[level_no], iterates[level_no] + prolong(iterates[level_no + 1]), face_sets[level_no], 0.25 ** level_no, zero_pad)
    solution = iterates[0]
    residual = right_side - apply_padded(zero_pad(solution), face_sets[0], 1.0)
    return solution, residual
```

```python
import functools

import jax
import jax.numpy as jnp
from jax import lax
from jax.experimental import pallas as pl
from jax.experimental.pallas import tpu as pltpu
from jax.sharding import PartitionSpec as P

DEGREE = 4
cheb_low = 0.3
cheb_high = 2.0
CENTRE = 0.5 * (cheb_high + cheb_low)
HALF = 0.5 * (cheb_high - cheb_low)
SIGMA = CENTRE / HALF
MESH = pl.DeviceIdType.MESH
CHUNKS = 2


def kernel(sizes, right_ref, coef_ref, sol_ref, res_ref, *scratch):
    (x0, x1, x2, g0, g1, g2, u0, u1, u2, b0, b1, b2, d0, d1, d2, hy, sy, hz, sz,
     relay_b, relay_k, send_sem, recv_sem, relay_send, relay_recv) = scratch
    xs, gs, us, bs, ds = (x0, x1, x2), (g0, g1, g2), (u0, u1, u2), (b0, b1, b2), (d0, d1, d2)
    size_gx, size_gy, size_gz = sizes
    half = size_gx // 2
    gx, gy, gz = lax.axis_index("gx"), lax.axis_index("gy"), lax.axis_index("gz")
    own = gx // half
    x = gx % half
    stages = relay_b.shape[0]
    reach = size_gy // stages

    def along_z(step):
        place = lax.rem(own * size_gy + gy + step + 2 * size_gy, 2 * size_gy)
        return ((place // size_gy) * half + x, lax.rem(place, size_gy), gz)

    x_right = (own * half + lax.rem(x + 1, half), gy, gz)
    x_left = (own * half + lax.rem(x + half - 1, half), gy, gz)
    y_up, y_down = (gx, gy + 1, gz), (gx, gy - 1, gz)
    z_up, z_down = (gx, gy, gz + 1), (gx, gy, gz - 1)
    has_y_up, has_y_down = gy < size_gy - 1, gy > 0
    has_z_up, has_z_down = gz < size_gz - 1, gz > 0
    optional = ((has_y_up, y_up), (has_y_down, y_down), (has_z_up, z_up), (has_z_down, z_down))

    def zero(ref):
        ref[...] = jnp.zeros_like(ref)

    for ref in (*xs, hy, sy, hz, sz):
        zero(ref)

    barrier = pltpu.get_barrier_semaphore()
    for device in (x_right, x_left, along_z(reach), along_z(-reach)):
        pl.semaphore_signal(barrier, inc=1, device_id=device, device_id_type=MESH)
    for there, device in optional:
        @pl.when(there)
        def _():
            pl.semaphore_signal(barrier, inc=1, device_id=device, device_id_type=MESH)
    count = 4
    for there, _ in optional:
        count = count + there.astype(jnp.int32)
    pl.semaphore_wait(barrier, count)

    part = 8 // CHUNKS

    def relay(stage, way, chunk):
        first, slots = ((right_ref, relay_b), (coef_ref, relay_k))[way]
        rows = pl.ds(chunk * part, part)
        source = first.at[rows] if stage == 0 else slots.at[stage - 1, rows]
        return pltpu.make_async_remote_copy(
            src_ref=source, dst_ref=slots.at[stage, rows],
            send_sem=relay_send.at[stage, way, chunk], recv_sem=relay_recv.at[stage, way, chunk],
            device_id=along_z(reach if way == 0 else -reach), device_id_type=MESH)

    for stage in range(stages):
        for chunk in range(CHUNKS):
            for way in range(2):
                if stage:
                    relay(stage - 1, way, chunk).wait_recv()
                relay(stage, way, chunk).start()
    for chunk in range(CHUNKS):
        for way in range(2):
            relay(stages - 1, way, chunk).wait_recv()
    for stage in range(stages):
        for chunk in range(CHUNKS):
            for way in range(2):
                relay(stage, way, chunk).wait_send()

    row = lax.broadcasted_iota(jnp.int32, (16, 128), 0)
    lane = lax.broadcasted_iota(jnp.int32, (16, 128), 1)

    def remote(level, par, index, source, target, device):
        return pltpu.make_async_remote_copy(
            src_ref=source, dst_ref=target, send_sem=send_sem.at[level, par, index[0]],
            recv_sem=recv_sem.at[level, par, index[1]], device_id=device, device_id_type=MESH)

    def planes(level):
        return xs[level].shape[2] - 2

    def copies(level, par):
        n = planes(level)
        buf = xs[level]
        over = (x == half - 1).astype(jnp.int32)
        under = (x > 0).astype(jnp.int32)
        used = max(8, 2 * n)
        rows = pl.ds(0, used)
        right = (
            (None, remote(level, par, (0, over), buf.at[par, 0, n], buf.at[par, over, 0], x_right)),
            (x < half - 1, remote(level, par, (1, 1), buf.at[par, 1, n], buf.at[par, 1, 0], x_right)),
            (None, remote(level, par, (2, 2 + under), buf.at[par, 1, 1], buf.at[par, under, n + 1], x_left)),
            (x > 0, remote(level, par, (3, 2), buf.at[par, 0, 1], buf.at[par, 0, n + 1], x_left)),
            (has_y_up, remote(level, par, (4, 4), sy.at[level, par, 0, rows], hy.at[level, par, 0, rows], y_up)),
            (has_y_down, remote(level, par, (5, 5), sy.at[level, par, 1, rows], hy.at[level, par, 1, rows], y_down)),
            (has_z_up, remote(level, par, (6, 6), sz.at[level, par, 0], hz.at[level, par, 0], z_up)),
            (has_z_down, remote(level, par, (7, 7), sz.at[level, par, 1], hz.at[level, par, 1], z_down)),
        )
        arrive = (
            (x > 0, remote(level, par, (0, 0), buf.at[par, 0, n], buf.at[par, 0, 0], x_right)),
            (None, remote(level, par, (1, 1), buf.at[par, 1, n], buf.at[par, 1, 0], x_right)),
            (None, remote(level, par, (3, 2), buf.at[par, 0, 1], buf.at[par, 0, n + 1], x_left)),
            (x < half - 1, remote(level, par, (2, 3), buf.at[par, 1, 1], buf.at[par, 1, n + 1], x_left)),
            (has_y_down, right[4][1]),
            (has_y_up, right[5][1]),
            (has_z_down, right[6][1]),
            (has_z_up, right[7][1]),
        )
        return right, arrive

    def each(listed, act):
        for there, copy in listed:
            if there is None:
                act(copy)
            else:
                @pl.when(there)
                def _():
                    act(copy)

    def start(level, par):
        n, w = planes(level), 2**level
        buf = xs[level]
        to_up, to_down = jnp.zeros((16, 128), jnp.float32), jnp.zeros((16, 128), jnp.float32)
        for s in range(2):
            sy[level, par, 0, s * n : (s + 1) * n, :] = buf[par, s, 1 : n + 1, 15, :]
            sy[level, par, 1, s * n : (s + 1) * n, :] = buf[par, s, 1 : n + 1, 0, :]
            for p in range(n):
                at = (s * n + p) * w
                here = (lane >= at) & (lane < at + w)
                value = buf[par, s, 1 + p]
                to_up = jnp.where(here, pltpu.roll(value, (at + w) % 128, 1), to_up)
                to_down = jnp.where(here, pltpu.roll(value, at, 1), to_down)
        sz[level, par, 0] = to_up
        sz[level, par, 1] = to_down
        each(copies(level, par)[0], lambda copy: copy.start())

    def finish(level, par):
        sent, arrive = copies(level, par)
        each(arrive, lambda copy: copy.wait_recv())
        each(sent, lambda copy: copy.wait_send())

    def neighbours(level, par, s):
        n, w = planes(level), 2**level
        buf = xs[level]
        value = buf[par, s, 1 : n + 1]
        low, high = hz[level, par, 0], hz[level, par, 1]
        shape = (n, 16, 128)
        lows = jnp.stack([pltpu.roll(low, (128 - (s * n + p) * w) % 128, 1) for p in range(n)])
        highs = jnp.stack([pltpu.roll(high, (128 - w - (s * n + p) * w) % 128, 1) for p in range(n)])
        under = jnp.broadcast_to(hy[level, par, 0, s * n : (s + 1) * n, :][:, None, :], shape)
        over = jnp.broadcast_to(hy[level, par, 1, s * n : (s + 1) * n, :][:, None, :], shape)
        return value, (
            buf[par, s, 0:n],
            buf[par, s, 2 : n + 2],
            jnp.where(row < w, under, pltpu.roll(value, w, 1)),
            jnp.where(row >= 16 - w, over, pltpu.roll(value, 16 - w, 1)),
            jnp.where(lane < w, lows, pltpu.roll(value, w, 2)),
            jnp.where(lane >= 128 - w, highs, pltpu.roll(value, 128 - w, 2)),
        )

    def scaled_residual(level, par, s):
        value, around = neighbours(level, par, s)
        total = bs[level][s] - value
        for i in range(6):
            total = total + gs[level][i, s] * around[i]
        return value, total

    def inside(level):
        return slice(1, planes(level) + 1)

    state = {"par": 0}

    def smooth(level, fresh):
        keep = inside(level)
        rho = 1.0 / SIGMA
        par = state["par"]
        if fresh:
            for s in range(2):
                u = bs[level][s] * (1.0 / CENTRE)
                us[level][s] = u
                xs[level][par, s, keep] = u
            sweeps = [None]
        else:
            sweeps = [(None, 1.0 / CENTRE)]
        sweeps = [] if fresh else [(0.0, 1.0 / CENTRE)]
        for _ in range(DEGREE - 1):
            rho_next = 1.0 / (2.0 * SIGMA - rho)
            sweeps.append((rho_next * rho, 2.0 * rho_next / HALF))
            rho = rho_next
        for old, new in sweeps:
            start(level, par)
            finish(level, par)
            for s in range(2):
                value, total = scaled_residual(level, par, s)
                u = new * total
                if old:
                    u = old * us[level][s] + u
                us[level][s] = u
                xs[level][1 - par, s, keep] = value + u
            par = 1 - par
        state["par"] = par

    def pair_sum(value, w):
        even_row = lax.rem(row, 2 * w) < w
        value = value + jnp.where(even_row, pltpu.roll(value, 16 - w, 1), pltpu.roll(value, w, 1))
        even_lane = lax.rem(lane, 2 * w) < w
        return value + jnp.where(even_lane, pltpu.roll(value, 128 - w, 2), pltpu.roll(value, w, 2))

    def restrict(value, w):
        total = pair_sum(value, w)
        return jnp.stack([total[2 * p] + total[2 * p + 1] for p in range(value.shape[0] // 2)]) * 0.125

    for level in range(3):
        n = planes(level)
        if level == 0:
            xs[0][0, own, 1 : n + 1] = coef_ref[...]
            xs[0][0, 1 - own, 1 : n + 1] = relay_k[stages - 1]
            bs[0][own] = right_ref[...]
            bs[0][1 - own] = relay_b[stages - 1]
        else:
            for s in range(2):
                xs[level][0, s, 1 : n + 1] = restrict(xs[level - 1][0, s, 1 : 2 * n + 1], 2 ** (level - 1))
        start(level, 0)
    for level in range(3):
        finish(level, 0)
        for s in range(2):
            value, around = neighbours(level, 0, s)
            faces = [0.5 * (value + other) for other in around]
            diagonal = faces[0]
            for face in faces[1:]:
                diagonal = diagonal + face
            inverse = 1.0 / diagonal
            for i in range(6):
                gs[level][i, s] = faces[i] * inverse
            ds[level][0, s] = diagonal * 0.25**level
            ds[level][1, s] = inverse * 4.0**level
    state["par"] = 1
    for s in range(2):
        bs[0][s] = bs[0][s] * ds[0][1, s]

    def down(level):
        par = state["par"]
        start(level, par)
        finish(level, par)
        for s in range(2):
            _, total = scaled_residual(level, par, s)
            coarse = restrict(total * ds[level][0, s], 2**level)
            bs[level + 1][s] = coarse * ds[level + 1][1, s]
        held = par
        state["par"] = 1 - par
        return held

    def correct(level, held):
        keep, coarse = inside(level), xs[level + 1]
        par = state["par"]
        for s in range(2):
            fine = xs[level][held, s, keep]
            add = coarse[par, s, inside(level + 1)]
            n = fine.shape[0] // 2
            wide = jnp.stack([add[p // 2] for p in range(2 * n)])
            xs[level][par, s, keep] = fine + wide

    smooth(0, True)
    held0 = down(0)
    smooth(1, True)
    held1 = down(1)
    smooth(2, True)
    correct(1, held1)
    smooth(1, False)
    correct(0, held0)
    smooth(0, False)
    par = state["par"]
    start(0, par)
    finish(0, par)
    for s in range(2):
        @pl.when(own == s)
        def _():
            value, total = scaled_residual(0, par, s)
            sol_ref[...] = value
            res_ref[...] = total * ds[0][0, s]


def solution(mesh):
    sizes = tuple(mesh.shape[a] for a in ("gx", "gy", "gz"))
    stages = 4 if sizes[1] % 4 == 0 else sizes[1]
    vmem = pltpu.VMEM
    f32 = jnp.float32
    levels = (8, 4, 2)
    scratch = (
        [vmem((2, 2, n + 2, 16, 128), f32) for n in levels]
        + [vmem((6, 2, n, 16, 128), f32) for n in levels]
        + [vmem((2, n, 16, 128), f32) for n in levels]
        + [vmem((2, n, 16, 128), f32) for n in levels]
        + [vmem((2, 2, n, 16, 128), f32) for n in levels]
        + [vmem((3, 2, 2, 16, 128), f32)] * 4
        + [vmem((stages, 8, 16, 128), f32)] * 2
        + [pltpu.SemaphoreType.DMA((3, 2, 8))] * 2
        + [pltpu.SemaphoreType.DMA((stages, 2, CHUNKS))] * 2
    )

    def per_device(right_side, coefficient):
        return pl.pallas_call(
            functools.partial(kernel, sizes),
            out_shape=(jax.ShapeDtypeStruct((8, 16, 128), f32),) * 2,
            in_specs=[pl.BlockSpec(memory_space=vmem)] * 2,
            out_specs=(pl.BlockSpec(memory_space=vmem),) * 2,
            scratch_shapes=scratch,
            compiler_params=pltpu.CompilerParams(collective_id=0, has_side_effects=True),
            name="vcycle",
        )(right_side, coefficient)

    specs = (P("gx", "gy", "gz"), P("gx", "gy", "gz"))
    return jax.shard_map(per_device, mesh=mesh, in_specs=specs, out_specs=specs, check_vma=False)
```

```python
import functools

import jax
import jax.numpy as jnp
from jax import lax
from jax.experimental import pallas as pl
from jax.experimental.pallas import tpu as pltpu
from jax.sharding import PartitionSpec as P

DEGREE = 4
cheb_low = 0.3
cheb_high = 2.0
CENTRE = 0.5 * (cheb_high + cheb_low)
HALF = 0.5 * (cheb_high - cheb_low)
SIGMA = CENTRE / HALF
MESH = pl.DeviceIdType.MESH
CHUNKS = 2


def kernel(sizes, right_ref, coef_ref, sol_ref, res_ref, *scratch):
    (x0, g0, u0, b0, d0, hy, sy, hz, sz, relay_b, relay_k, send_sem, recv_sem, relay_send, relay_recv,
     k1, r1, x1a, x1b, x1s, g1, u1, d1, k2, r2, x2a, x2b, g2, u2, d2, wide, zs, zr,
     gather_send, gather_recv, cross_send, cross_recv) = scratch
    xs, gs, us, bs, ds = (x0,), (g0,), (u0,), (b0,), (d0,)
    size_gx, size_gy, size_gz = sizes
    half = size_gx // 2
    gx, gy, gz = lax.axis_index("gx"), lax.axis_index("gy"), lax.axis_index("gz")
    own = gx // half
    x = gx % half
    stages = relay_b.shape[0]
    reach = size_gy // stages

    def along_z(step):
        place = lax.rem(own * size_gy + gy + step + 2 * size_gy, 2 * size_gy)
        return ((place // size_gy) * half + x, lax.rem(place, size_gy), gz)

    x_right = (own * half + lax.rem(x + 1, half), gy, gz)
    x_left = (own * half + lax.rem(x + half - 1, half), gy, gz)
    y_up, y_down = (gx, gy + 1, gz), (gx, gy - 1, gz)
    z_up, z_down = (gx, gy, gz + 1), (gx, gy, gz - 1)
    has_y_up, has_y_down = gy < size_gy - 1, gy > 0
    has_z_up, has_z_down = gz < size_gz - 1, gz > 0
    optional = ((has_y_up, y_up), (has_y_down, y_down), (has_z_up, z_up), (has_z_down, z_down))

    def zero(ref):
        ref[...] = jnp.zeros_like(ref)

    for ref in (*xs, hy, sy, hz, sz, k1, r1, x1s, r2, zs, zr):
        zero(ref)

    barrier = pltpu.get_barrier_semaphore()
    for device in (x_right, x_left, along_z(reach), along_z(-reach)):
        pl.semaphore_signal(barrier, inc=1, device_id=device, device_id_type=MESH)
    corners = (
        (has_y_up & has_z_up, (gx, gy + 1, gz + 1)),
        (has_y_up & has_z_down, (gx, gy + 1, gz - 1)),
        (has_y_down & has_z_up, (gx, gy - 1, gz + 1)),
        (has_y_down & has_z_down, (gx, gy - 1, gz - 1)),
    )
    for there, device in (*optional, *corners):
        @pl.when(there)
        def _():
            pl.semaphore_signal(barrier, inc=1, device_id=device, device_id_type=MESH)
    count = 2 + max(half - 1, 2)
    for step in range(2, half - 1):
        device = (own * half + lax.rem(x + step, half), gy, gz)
        pl.semaphore_signal(barrier, inc=1, device_id=device, device_id_type=MESH)
    for there, _ in (*optional, *corners):
        count = count + there.astype(jnp.int32)
    pl.semaphore_wait(barrier, count)

    part = 8 // CHUNKS

    def relay(stage, way, chunk):
        first, slots = ((right_ref, relay_b), (coef_ref, relay_k))[way]
        rows = pl.ds(chunk * part, part)
        source = first.at[rows] if stage == 0 else slots.at[stage - 1, rows]
        return pltpu.make_async_remote_copy(
            src_ref=source, dst_ref=slots.at[stage, rows],
            send_sem=relay_send.at[stage, way, chunk], recv_sem=relay_recv.at[stage, way, chunk],
            device_id=along_z(reach if way == 0 else -reach), device_id_type=MESH)

    for stage in range(stages):
        for chunk in range(CHUNKS):
            for way in range(2):
                if stage:
                    relay(stage - 1, way, chunk).wait_recv()
                relay(stage, way, chunk).start()
    for chunk in range(CHUNKS):
        for way in range(2):
            relay(stages - 1, way, chunk).wait_recv()
    for stage in range(stages):
        for chunk in range(CHUNKS):
            for way in range(2):
                relay(stage, way, chunk).wait_send()

    row = lax.broadcasted_iota(jnp.int32, (16, 128), 0)
    lane = lax.broadcasted_iota(jnp.int32, (16, 128), 1)

    def remote(level, par, index, source, target, device):
        return pltpu.make_async_remote_copy(
            src_ref=source, dst_ref=target, send_sem=send_sem.at[level, par, index[0]],
            recv_sem=recv_sem.at[level, par, index[1]], device_id=device, device_id_type=MESH)

    def planes(level):
        return xs[level].shape[2] - 2

    def copies(level, par):
        n = planes(level)
        buf = xs[level]
        over = (x == half - 1).astype(jnp.int32)
        under = (x > 0).astype(jnp.int32)
        used = max(8, 2 * n)
        rows = pl.ds(0, used)
        right = (
            (None, remote(level, par, (0, over), buf.at[par, 0, n], buf.at[par, over, 0], x_right)),
            (x < half - 1, remote(level, par, (1, 1), buf.at[par, 1, n], buf.at[par, 1, 0], x_right)),
            (None, remote(level, par, (2, 2 + under), buf.at[par, 1, 1], buf.at[par, under, n + 1], x_left)),
            (x > 0, remote(level, par, (3, 2), buf.at[par, 0, 1], buf.at[par, 0, n + 1], x_left)),
            (has_y_up, remote(level, par, (4, 4), sy.at[level, par, 0, rows], hy.at[level, par, 0, rows], y_up)),
            (has_y_down, remote(level, par, (5, 5), sy.at[level, par, 1, rows], hy.at[level, par, 1, rows], y_down)),
            (has_z_up, remote(level, par, (6, 6), sz.at[level, par, 0], hz.at[level, par, 0], z_up)),
            (has_z_down, remote(level, par, (7, 7), sz.at[level, par, 1], hz.at[level, par, 1], z_down)),
        )
        arrive = (
            (x > 0, remote(level, par, (0, 0), buf.at[par, 0, n], buf.at[par, 0, 0], x_right)),
            (None, remote(level, par, (1, 1), buf.at[par, 1, n], buf.at[par, 1, 0], x_right)),
            (None, remote(level, par, (3, 2), buf.at[par, 0, 1], buf.at[par, 0, n + 1], x_left)),
            (x < half - 1, remote(level, par, (2, 3), buf.at[par, 1, 1], buf.at[par, 1, n + 1], x_left)),
            (has_y_down, right[4][1]),
            (has_y_up, right[5][1]),
            (has_z_down, right[6][1]),
            (has_z_up, right[7][1]),
        )
        return right, arrive

    def each(listed, act):
        for there, copy in listed:
            if there is None:
                act(copy)
            else:
                @pl.when(there)
                def _():
                    act(copy)

    def start(level, par):
        n, w = planes(level), 2**level
        buf = xs[level]
        to_up, to_down = jnp.zeros((16, 128), jnp.float32), jnp.zeros((16, 128), jnp.float32)
        for s in range(2):
            sy[level, par, 0, s * n : (s + 1) * n, :] = buf[par, s, 1 : n + 1, 15, :]
            sy[level, par, 1, s * n : (s + 1) * n, :] = buf[par, s, 1 : n + 1, 0, :]
            for p in range(n):
                at = (s * n + p) * w
                here = (lane >= at) & (lane < at + w)
                value = buf[par, s, 1 + p]
                to_up = jnp.where(here, pltpu.roll(value, (at + w) % 128, 1), to_up)
                to_down = jnp.where(here, pltpu.roll(value, at, 1), to_down)
        sz[level, par, 0] = to_up
        sz[level, par, 1] = to_down
        each(copies(level, par)[0], lambda copy: copy.start())

    def finish(level, par):
        sent, arrive = copies(level, par)
        each(arrive, lambda copy: copy.wait_recv())
        each(sent, lambda copy: copy.wait_send())

    def neighbours(level, par, s):
        n, w = planes(level), 2**level
        buf = xs[level]
        value = buf[par, s, 1 : n + 1]
        low, high = hz[level, par, 0], hz[level, par, 1]
        shape = (n, 16, 128)
        lows = jnp.stack([pltpu.roll(low, (128 - (s * n + p) * w) % 128, 1) for p in range(n)])
        highs = jnp.stack([pltpu.roll(high, (128 - w - (s * n + p) * w) % 128, 1) for p in range(n)])
        under = jnp.broadcast_to(hy[level, par, 0, s * n : (s + 1) * n, :][:, None, :], shape)
        over = jnp.broadcast_to(hy[level, par, 1, s * n : (s + 1) * n, :][:, None, :], shape)
        return value, (
            buf[par, s, 0:n],
            buf[par, s, 2 : n + 2],
            jnp.where(row < w, under, pltpu.roll(value, w, 1)),
            jnp.where(row >= 16 - w, over, pltpu.roll(value, 16 - w, 1)),
            jnp.where(lane < w, lows, pltpu.roll(value, w, 2)),
            jnp.where(lane >= 128 - w, highs, pltpu.roll(value, 128 - w, 2)),
        )

    def scaled_residual(level, par, s):
        value, around = neighbours(level, par, s)
        total = bs[level][s] - value
        for i in range(6):
            total = total + gs[level][i, s] * around[i]
        return value, total

    def inside(level):
        return slice(1, planes(level) + 1)

    state = {"par": 0}

    def smooth(level, fresh, between=None):
        keep = inside(level)
        rho = 1.0 / SIGMA
        par = state["par"]
        if fresh:
            for s in range(2):
                u = bs[level][s] * (1.0 / CENTRE)
                us[level][s] = u
                xs[level][par, s, keep] = u
        sweeps = [] if fresh else [(0.0, 1.0 / CENTRE)]
        for _ in range(DEGREE - 1):
            rho_next = 1.0 / (2.0 * SIGMA - rho)
            sweeps.append((rho_next * rho, 2.0 * rho_next / HALF))
            rho = rho_next
        for number, (old, new) in enumerate(sweeps):
            start(level, par)
            if between:
                between(number)
            finish(level, par)
            for s in range(2):
                value, total = scaled_residual(level, par, s)
                u = new * total
                if old:
                    u = old * us[level][s] + u
                us[level][s] = u
                xs[level][1 - par, s, keep] = value + u
            par = 1 - par
        state["par"] = par

    def pair_sum(value, w):
        even_row = lax.rem(row, 2 * w) < w
        value = value + jnp.where(even_row, pltpu.roll(value, 16 - w, 1), pltpu.roll(value, w, 1))
        even_lane = lax.rem(lane, 2 * w) < w
        return value + jnp.where(even_lane, pltpu.roll(value, 128 - w, 2), pltpu.roll(value, w, 2))

    def restrict(value, w):
        total = pair_sum(value, w)
        return jnp.stack([total[2 * p] + total[2 * p + 1] for p in range(value.shape[0] // 2)]) * 0.125

    count1, count2 = 4 * half, 2 * half
    wide_row = lax.broadcasted_iota(jnp.int32, (24, 256), 0)
    wide_lane = lax.broadcasted_iota(jnp.int32, (24, 256), 1)
    odd = lax.rem(wide_lane, 2) == 1
    lane8 = lax.broadcasted_iota(jnp.int32, (8, 128), 1)
    odd8 = lax.rem(lane8, 2) == 1
    mine, owned = slice(0, 8), slice(0, 128)

    def gather_copy(which, ref, base, step):
        part_of = pl.ds(base + 4 * x, 4)
        return pltpu.make_async_remote_copy(
            src_ref=ref.at[part_of, mine, owned], dst_ref=ref.at[part_of, mine, owned],
            send_sem=gather_send.at[which, step], recv_sem=gather_recv.at[which, step],
            device_id=(own * half + lax.rem(x + step, half), gy, gz), device_id_type=MESH)

    def gather_start(which, ref, base, values):
        for s in range(2):
            wide[s] = values[s]
        for p in range(4):
            low, high = wide[0, p, pl.ds(0, 8, stride=2), :], wide[1, p, pl.ds(0, 8, stride=2), :]
            ref[base + 4 * x + p, mine, owned] = jnp.where(odd8, high, low)
        for step in range(1, half):
            gather_copy(which, ref, base, step).start()

    def gather_finish(which, ref, base):
        for step in range(1, half):
            source = lax.rem(x + half - step, half)
            part_of = pl.ds(base + 4 * source, 4)
            pltpu.make_async_remote_copy(
                src_ref=ref.at[part_of, mine, owned], dst_ref=ref.at[part_of, mine, owned],
                send_sem=gather_send.at[which, step], recv_sem=gather_recv.at[which, step],
                device_id=(own * half + lax.rem(x + step, half), gy, gz), device_id_type=MESH).wait_recv()
        for step in range(1, half):
            gather_copy(which, ref, base, step).wait_send()

    def cross_copies(stage, ref, base, number):
        tiles = pl.ds(0, max(1, number // 8))
        body = slice(base, base + number)

        def to(index, source, target, device):
            return pltpu.make_async_remote_copy(
                src_ref=source, dst_ref=target, send_sem=cross_send.at[stage, index],
                recv_sem=cross_recv.at[stage, index], device_id=device, device_id_type=MESH)

        def pack(index, side, block, device):
            return to(index, zs.at[stage, side, tiles], zr.at[stage, side, block, tiles], device)

        block = ref.at[body, mine, owned]
        sent = (
            (has_y_up, to(0, block, ref.at[body, 16:24, owned], y_up)),
            (has_y_down, to(1, block, ref.at[body, 8:16, owned], y_down)),
            (has_z_up, pack(2, 0, 0, z_up)),
            (has_z_down, pack(3, 1, 0, z_down)),
            (corners[0][0], pack(4, 0, 2, corners[0][1])),
            (corners[1][0], pack(5, 1, 2, corners[1][1])),
            (corners[2][0], pack(6, 0, 1, corners[2][1])),
            (corners[3][0], pack(7, 1, 1, corners[3][1])),
        )
        opposite = (has_y_down, has_y_up, has_z_down, has_z_up,
                    corners[3][0], corners[2][0], corners[1][0], corners[0][0])
        arrive = tuple((there, sent[i][1]) for i, there in enumerate(opposite))
        return sent, arrive

    def cross_start(stage, ref, base, number):
        for t in range(max(1, number // 8)):
            high, low = jnp.zeros((8, 128), jnp.float32), jnp.zeros((8, 128), jnp.float32)
            for i in range(min(8, number)):
                value = ref[base + 8 * t + i, mine, owned]
                here = (lane8 >= 16 * i) & (lane8 < 16 * i + 16)
                high = jnp.where(here, pltpu.roll(value, (16 * i + 16) % 128, 1), high)
                low = jnp.where(here, pltpu.roll(value, 16 * i, 1), low)
            zs[stage, 0, t] = high
            zs[stage, 1, t] = low
        each(cross_copies(stage, ref, base, number)[0], lambda copy: copy.start())

    def cross_finish(stage, ref, base, number):
        sent, arrive = cross_copies(stage, ref, base, number)
        each(arrive, lambda copy: copy.wait_recv())
        each(sent, lambda copy: copy.wait_send())
        for t in range(max(1, number // 8)):
            for block in range(3):
                below, above = zr[stage, 0, block, t], zr[stage, 1, block, t]
                for i in range(min(8, number)):
                    ref[base + 8 * t + i, 8 * block : 8 * block + 8, 128:256] = jnp.where(
                        lane8 < 16, pltpu.roll(above, (128 - 16 * i) % 128, 1),
                        jnp.where(lane8 >= 112, pltpu.roll(below, (112 - 16 * i) % 128, 1), 0.0))

    def edges(ref, number):
        ref[0] = jnp.where(odd, pltpu.roll(ref[number], 1, 1), 0.0)
        ref[number + 1] = jnp.where(odd, 0.0, pltpu.roll(ref[1], 255, 1))

    GROUP = 2

    def groups(number):
        return [(a, a + GROUP) for a in range(0, number, GROUP)]

    def spread(ref, a, b, level):
        w = level
        value = ref[1 + a : 1 + b]
        return value, (
            ref[a:b], ref[a + 2 : b + 2],
            pltpu.roll(value, w, 1), pltpu.roll(value, 24 - w, 1),
            pltpu.roll(value, 2 * w, 2), pltpu.roll(value, 256 - 2 * w, 2),
        )

    def coarse_faces(level, ref, number, gref, dref):
        edges(ref, number)
        for a, b in groups(number):
            value, around = spread(ref, a, b, level)
            faces = [0.5 * (value + other) for other in around]
            diagonal = faces[0]
            for face in faces[1:]:
                diagonal = diagonal + face
            inverse = jnp.where(value > 0.0, 1.0 / diagonal, 0.0)
            for i in range(6):
                gref[i, a:b] = faces[i] * inverse
            dref[0, a:b] = diagonal * 0.25**level
            dref[1, a:b] = inverse * 4.0**level

    def coarse_total(level, ref, a, b, right, gref):
        value, around = spread(ref, a, b, level)
        total = right[a:b] - value
        for i in range(6):
            total = total + gref[i, a:b] * around[i]
        return value, total

    def coarse_smooth(level, begin, buffers, number, right, gref, uref):
        rho = 1.0 / SIGMA
        now, sweeps = begin, []
        if begin is None:
            now, buffers = buffers[0], buffers[1:] + buffers[:1]
            for a, b in groups(number):
                u = right[a:b] * (1.0 / CENTRE)
                uref[a:b] = u
                now[1 + a : 1 + b] = u
        else:
            sweeps = [(0.0, 1.0 / CENTRE)]
        for _ in range(DEGREE - 1):
            rho_next = 1.0 / (2.0 * SIGMA - rho)
            sweeps.append((rho_next * rho, 2.0 * rho_next / HALF))
            rho = rho_next
        for old, new in sweeps:
            then, buffers = buffers[0], buffers[1:] + buffers[:1]
            edges(now, number)
            for a, b in groups(number):
                value, total = coarse_total(level, now, a, b, right, gref)
                u = new * total
                if old:
                    u = old * uref[a:b] + u
                uref[a:b] = u
                then[1 + a : 1 + b] = value + u
            now = then
        return now

    def coarse_restrict(pairs):
        value = pairs[0] + pairs[1]
        value = value + jnp.where(lax.rem(wide_row, 2) == 0, pltpu.roll(value, 23, 0), pltpu.roll(value, 1, 0))
        value = value + jnp.where(lax.rem(wide_lane, 4) < 2, pltpu.roll(value, 254, 1), pltpu.roll(value, 2, 1))
        return value * 0.125

    xs[0][0, own, 1:9] = coef_ref[...]
    xs[0][0, 1 - own, 1:9] = relay_k[stages - 1]
    bs[0][own] = right_ref[...]
    bs[0][1 - own] = relay_b[stages - 1]
    start(0, 0)
    gather_start(0, k1, 1, [restrict(xs[0][0, s, 1:9], 1) for s in range(2)])
    finish(0, 0)
    for s in range(2):
        value, around = neighbours(0, 0, s)
        faces = [0.5 * (value + other) for other in around]
        diagonal = faces[0]
        for face in faces[1:]:
            diagonal = diagonal + face
        inverse = 1.0 / diagonal
        for i in range(6):
            gs[0][i, s] = faces[i] * inverse
        ds[0][0, s] = diagonal
        ds[0][1, s] = inverse
        bs[0][s] = bs[0][s] * inverse
    state["par"] = 1

    def between(sweep):
        if sweep == 0:
            gather_finish(0, k1, 1)
            cross_start(0, k1, 1, count1)
        if sweep == 1:
            cross_finish(0, k1, 1, count1)
            coarse_faces(1, k1, count1, g1, d1)
        if sweep == 2:
            for m in range(count2):
                k2[1 + m] = coarse_restrict(k1[1 + 2 * m : 3 + 2 * m])
            coarse_faces(2, k2, count2, g2, d2)

    smooth(0, True, between)
    held = state["par"]
    start(0, held)
    finish(0, held)
    fine = []
    for s in range(2):
        _, total = scaled_residual(0, held, s)
        fine.append(restrict(total * ds[0][0, s], 1))
    gather_start(1, r1, 0, fine)
    gather_finish(1, r1, 0)
    cross_start(1, r1, 0, count1)
    cross_finish(1, r1, 0, count1)
    for a, b in groups(count1):
        r1[a:b] = r1[a:b] * d1[1, a:b]
    now = coarse_smooth(1, None, [x1a, x1b], count1, r1, g1, u1)
    edges(now, count1)
    for m in range(count2):
        _, total = coarse_total(1, now, 2 * m, 2 * m + 2, r1, g1)
        r2[m, mine, owned] = coarse_restrict(total * d1[0, 2 * m : 2 * m + 2])[mine, owned]
    cross_start(2, r2, 0, count2)
    cross_finish(2, r2, 0, count2)
    for a, b in groups(count2):
        r2[a:b] = r2[a:b] * d2[1, a:b]
    deep = coarse_smooth(2, None, [x2a, x2b], count2, r2, g2, u2)
    for q in range(count1):
        x1s[1 + q, mine, owned] = now[1 + q, mine, owned] + deep[1 + q // 2, mine, owned]
    cross_start(3, x1s, 1, count1)
    cross_finish(3, x1s, 1, count1)
    now = coarse_smooth(1, x1s, [x1a, x1b], count1, r1, g1, u1)
    par = 1 - held
    for p in range(4):
        value = now[1 + 4 * x + p, mine, owned]
        for s in range(2):
            half_of = jnp.where(odd8, value, pltpu.roll(value, 127, 1)) if s else jnp.where(odd8, pltpu.roll(value, 1, 1), value)
            wide[s, p, pl.ds(0, 8, stride=2), :] = half_of
            wide[s, p, pl.ds(1, 8, stride=2), :] = half_of
    for s in range(2):
        for p in range(8):
            xs[0][par, s, 1 + p] = xs[0][held, s, 1 + p] + wide[s, p // 2]
    state["par"] = par
    smooth(0, False)
    par = state["par"]
    start(0, par)
    finish(0, par)
    for s in range(2):
        @pl.when(own == s)
        def _():
            value, total = scaled_residual(0, par, s)
            sol_ref[...] = value
            res_ref[...] = total * ds[0][0, s]


def solution(mesh):
    sizes = tuple(mesh.shape[a] for a in ("gx", "gy", "gz"))
    stages = 4 if sizes[1] % 4 == 0 else sizes[1]
    vmem = pltpu.VMEM
    f32 = jnp.float32
    half = sizes[0] // 2
    n1, n2 = 4 * half, 2 * half
    dma = pltpu.SemaphoreType.DMA

    def big(*lead):
        return vmem((*lead, 24, 256), f32)

    scratch = [
        vmem((2, 2, 10, 16, 128), f32), vmem((6, 2, 8, 16, 128), f32), vmem((2, 8, 16, 128), f32),
        vmem((2, 8, 16, 128), f32), vmem((2, 2, 8, 16, 128), f32),
        *[vmem((1, 2, 2, 16, 128), f32)] * 4,
        *[vmem((stages, 8, 16, 128), f32)] * 2,
        *[dma((1, 2, 8))] * 2, *[dma((stages, 2, CHUNKS))] * 2,
        big(n1 + 2), big(n1), big(n1 + 2), big(n1 + 2), big(n1 + 2), big(6, n1), big(n1), big(2, n1),
        big(n2 + 2), big(n2), big(n2 + 2), big(n2 + 2), big(6, n2), big(n2), big(2, n2),
        vmem((2, 4, 16, 128), f32), vmem((4, 2, 2, 8, 128), f32), vmem((4, 2, 3, 2, 8, 128), f32),
        *[dma((2, half))] * 2, *[dma((4, 8))] * 2,
    ]

    def per_device(right_side, coefficient):
        return pl.pallas_call(
            functools.partial(kernel, sizes),
            out_shape=(jax.ShapeDtypeStruct((8, 16, 128), f32),) * 2,
            in_specs=[pl.BlockSpec(memory_space=vmem)] * 2,
            out_specs=(pl.BlockSpec(memory_space=vmem),) * 2,
            scratch_shapes=scratch,
            compiler_params=pltpu.CompilerParams(collective_id=0, has_side_effects=True),
            name="vcycle",
        )(right_side, coefficient)

    specs = (P("gx", "gy", "gz"), P("gx", "gy", "gz"))
    return jax.shard_map(per_device, mesh=mesh, in_specs=specs, out_specs=specs, check_vma=False)
```

```python
import functools

import jax
import jax.numpy as jnp
from jax import lax
from jax.experimental import pallas as pl
from jax.experimental.pallas import tpu as pltpu
from jax.sharding import PartitionSpec as P

DEGREE = 4
cheb_low = 0.3
cheb_high = 2.0
CENTRE = 0.5 * (cheb_high + cheb_low)
HALF = 0.5 * (cheb_high - cheb_low)
SIGMA = CENTRE / HALF
MESH = pl.DeviceIdType.MESH


def kernel(sizes, right_ref, coef_ref, sol_ref, res_ref, *scratch):
    (x0, g0, u0, b0, d0, hy, sy, hz, sz, relay_b, relay_k, send_sem, recv_sem, relay_send, relay_recv,
     k1, r1, x1a, x1b, x1s, g1, u1, d1, k2, r2, x2a, x2b, g2, u2, d2, wide, zs, zr,
     gather_send, gather_recv, cross_send, cross_recv,
     ek, eb, exa, exb, eg, eu, ez, er, side_send, side_recv, deep_send, deep_recv, spill) = scratch
    xs, gs, us, bs, ds = (x0,), (g0,), (u0,), (b0,), (d0,)
    size_gx, size_gy, size_gz = sizes
    half = size_gx // 2
    gx, gy, gz = lax.axis_index("gx"), lax.axis_index("gy"), lax.axis_index("gz")
    own = gx // half
    x = gx % half

    across = ((1 - own) * half + x, gy, gz)

    x_right = (own * half + lax.rem(x + 1, half), gy, gz)
    x_left = (own * half + lax.rem(x + half - 1, half), gy, gz)
    y_up, y_down = (gx, gy + 1, gz), (gx, gy - 1, gz)
    z_up, z_down = (gx, gy, gz + 1), (gx, gy, gz - 1)
    has_y_up, has_y_down = gy < size_gy - 1, gy > 0
    has_z_up, has_z_down = gz < size_gz - 1, gz > 0
    optional = ((has_y_up, y_up), (has_y_down, y_down), (has_z_up, z_up), (has_z_down, z_down))

    def zero(ref):
        ref[...] = jnp.zeros_like(ref)

    for ref in (*xs, hy, sy, hz, sz, k1, r1, x1s, r2, zs, zr, ek, eb, exa, er):
        zero(ref)

    barrier = pltpu.get_barrier_semaphore()
    for device in (x_right, x_left, across):
        pl.semaphore_signal(barrier, inc=1, device_id=device, device_id_type=MESH)
    corners = (
        (has_y_up & has_z_up, (gx, gy + 1, gz + 1)),
        (has_y_up & has_z_down, (gx, gy + 1, gz - 1)),
        (has_y_down & has_z_up, (gx, gy - 1, gz + 1)),
        (has_y_down & has_z_down, (gx, gy - 1, gz - 1)),
    )
    for there, device in (*optional, *corners):
        @pl.when(there)
        def _():
            pl.semaphore_signal(barrier, inc=1, device_id=device, device_id_type=MESH)
    count = 1 + max(half - 1, 2)
    for step in range(2, half - 1):
        device = (own * half + lax.rem(x + step, half), gy, gz)
        pl.semaphore_signal(barrier, inc=1, device_id=device, device_id_type=MESH)
    for there, _ in (*optional, *corners):
        count = count + there.astype(jnp.int32)
    pl.semaphore_wait(barrier, count)

    def swap(which):
        source, target = ((coef_ref, relay_k), (right_ref, relay_b))[which]
        return pltpu.make_async_remote_copy(
            src_ref=source, dst_ref=target, send_sem=relay_send.at[which], recv_sem=relay_recv.at[which],
            device_id=across, device_id_type=MESH)

    swap(0).start()
    swap(1).start()
    swap(0).wait()

    row = lax.broadcasted_iota(jnp.int32, (16, 128), 0)
    lane = lax.broadcasted_iota(jnp.int32, (16, 128), 1)

    def remote(level, par, index, source, target, device):
        return pltpu.make_async_remote_copy(
            src_ref=source, dst_ref=target, send_sem=send_sem.at[level, par, index[0]],
            recv_sem=recv_sem.at[level, par, index[1]], device_id=device, device_id_type=MESH)

    def planes(level):
        return xs[level].shape[2] - 2

    def copies(level, par):
        n = planes(level)
        buf = xs[level]
        over = (x == half - 1).astype(jnp.int32)
        under = (x > 0).astype(jnp.int32)
        used = max(8, 2 * n)
        rows = pl.ds(0, used)
        right = (
            (None, remote(level, par, (0, over), buf.at[par, 0, n], buf.at[par, over, 0], x_right)),
            (x < half - 1, remote(level, par, (1, 1), buf.at[par, 1, n], buf.at[par, 1, 0], x_right)),
            (None, remote(level, par, (2, 2 + under), buf.at[par, 1, 1], buf.at[par, under, n + 1], x_left)),
            (x > 0, remote(level, par, (3, 2), buf.at[par, 0, 1], buf.at[par, 0, n + 1], x_left)),
            (has_y_up, remote(level, par, (4, 4), sy.at[level, par, 0, rows], hy.at[level, par, 0, rows], y_up)),
            (has_y_down, remote(level, par, (5, 5), sy.at[level, par, 1, rows], hy.at[level, par, 1, rows], y_down)),
            (has_z_up, remote(level, par, (6, 6), sz.at[level, par, 0], hz.at[level, par, 0], z_up)),
            (has_z_down, remote(level, par, (7, 7), sz.at[level, par, 1], hz.at[level, par, 1], z_down)),
        )
        arrive = (
            (x > 0, remote(level, par, (0, 0), buf.at[par, 0, n], buf.at[par, 0, 0], x_right)),
            (None, remote(level, par, (1, 1), buf.at[par, 1, n], buf.at[par, 1, 0], x_right)),
            (None, remote(level, par, (3, 2), buf.at[par, 0, 1], buf.at[par, 0, n + 1], x_left)),
            (x < half - 1, remote(level, par, (2, 3), buf.at[par, 1, 1], buf.at[par, 1, n + 1], x_left)),
            (has_y_down, right[4][1]),
            (has_y_up, right[5][1]),
            (has_z_down, right[6][1]),
            (has_z_up, right[7][1]),
        )
        return right, arrive

    def each(listed, act):
        for there, copy in listed:
            if there is None:
                act(copy)
            else:
                @pl.when(there)
                def _():
                    act(copy)

    def start(level, par):
        n, w = planes(level), 2**level
        buf = xs[level]
        to_up, to_down = jnp.zeros((16, 128), jnp.float32), jnp.zeros((16, 128), jnp.float32)
        for s in range(2):
            sy[level, par, 0, s * n : (s + 1) * n, :] = buf[par, s, 1 : n + 1, 15, :]
            sy[level, par, 1, s * n : (s + 1) * n, :] = buf[par, s, 1 : n + 1, 0, :]
            for p in range(n):
                at = (s * n + p) * w
                here = (lane >= at) & (lane < at + w)
                value = buf[par, s, 1 + p]
                to_up = jnp.where(here, pltpu.roll(value, (at + w) % 128, 1), to_up)
                to_down = jnp.where(here, pltpu.roll(value, at, 1), to_down)
        sz[level, par, 0] = to_up
        sz[level, par, 1] = to_down
        each(copies(level, par)[0], lambda copy: copy.start())

    def finish(level, par):
        sent, arrive = copies(level, par)
        each(arrive, lambda copy: copy.wait_recv())
        each(sent, lambda copy: copy.wait_send())

    def neighbours(level, par, s):
        n, w = planes(level), 2**level
        buf = xs[level]
        value = buf[par, s, 1 : n + 1]
        low, high = hz[level, par, 0], hz[level, par, 1]
        shape = (n, 16, 128)
        lows = jnp.stack([pltpu.roll(low, (128 - (s * n + p) * w) % 128, 1) for p in range(n)])
        highs = jnp.stack([pltpu.roll(high, (128 - w - (s * n + p) * w) % 128, 1) for p in range(n)])
        under = jnp.broadcast_to(hy[level, par, 0, s * n : (s + 1) * n, :][:, None, :], shape)
        over = jnp.broadcast_to(hy[level, par, 1, s * n : (s + 1) * n, :][:, None, :], shape)
        return value, (
            buf[par, s, 0:n],
            buf[par, s, 2 : n + 2],
            jnp.where(row < w, under, pltpu.roll(value, w, 1)),
            jnp.where(row >= 16 - w, over, pltpu.roll(value, 16 - w, 1)),
            jnp.where(lane < w, lows, pltpu.roll(value, w, 2)),
            jnp.where(lane >= 128 - w, highs, pltpu.roll(value, 128 - w, 2)),
        )

    def scaled_residual(level, par, s):
        value, around = neighbours(level, par, s)
        total = bs[level][s] - value
        for i in range(6):
            total = total + gs[level][i, s] * around[i]
        return value, total

    def inside(level):
        return slice(1, planes(level) + 1)

    state = {"par": 0}

    def smooth(level, fresh, between=None):
        keep = inside(level)
        rho = 1.0 / SIGMA
        par = state["par"]
        if fresh:
            for s in range(2):
                u = bs[level][s] * (1.0 / CENTRE)
                us[level][s] = u
                xs[level][par, s, keep] = u
        sweeps = [] if fresh else [(0.0, 1.0 / CENTRE)]
        for _ in range(DEGREE - 1):
            rho_next = 1.0 / (2.0 * SIGMA - rho)
            sweeps.append((rho_next * rho, 2.0 * rho_next / HALF))
            rho = rho_next
        for number, (old, new) in enumerate(sweeps):
            start(level, par)
            if between:
                between(number)
            finish(level, par)
            for s in range(2):
                value, total = scaled_residual(level, par, s)
                u = new * total
                if old:
                    u = old * us[level][s] + u
                us[level][s] = u
                xs[level][1 - par, s, keep] = value + u
            par = 1 - par
        state["par"] = par

    def pair_sum(value, w):
        even_row = lax.rem(row, 2 * w) < w
        value = value + jnp.where(even_row, pltpu.roll(value, 16 - w, 1), pltpu.roll(value, w, 1))
        even_lane = lax.rem(lane, 2 * w) < w
        return value + jnp.where(even_lane, pltpu.roll(value, 128 - w, 2), pltpu.roll(value, w, 2))

    def restrict(value, w):
        total = pair_sum(value, w)
        return jnp.stack([total[2 * p] + total[2 * p + 1] for p in range(value.shape[0] // 2)]) * 0.125

    count1, count2 = 4 * half, 2 * half
    wide_row = lax.broadcasted_iota(jnp.int32, (24, 256), 0)
    wide_lane = lax.broadcasted_iota(jnp.int32, (24, 256), 1)
    odd = lax.rem(wide_lane, 2) == 1
    lane8 = lax.broadcasted_iota(jnp.int32, (8, 128), 1)
    odd8 = lax.rem(lane8, 2) == 1
    mine, owned = slice(0, 8), slice(0, 128)

    def gather_copy(which, ref, base, step):
        part_of = pl.ds(base + 4 * x, 4)
        return pltpu.make_async_remote_copy(
            src_ref=ref.at[part_of, mine, owned], dst_ref=ref.at[part_of, mine, owned],
            send_sem=gather_send.at[which, step], recv_sem=gather_recv.at[which, step],
            device_id=(own * half + lax.rem(x + step, half), gy, gz), device_id_type=MESH)

    def gather_start(which, ref, base, values):
        for s in range(2):
            wide[s] = values[s]
        for p in range(4):
            low, high = wide[0, p, pl.ds(0, 8, stride=2), :], wide[1, p, pl.ds(0, 8, stride=2), :]
            ref[base + 4 * x + p, mine, owned] = jnp.where(odd8, high, low)
        for step in range(1, half):
            gather_copy(which, ref, base, step).start()

    def gather_finish(which, ref, base):
        for step in range(1, half):
            source = lax.rem(x + half - step, half)
            part_of = pl.ds(base + 4 * source, 4)
            pltpu.make_async_remote_copy(
                src_ref=ref.at[part_of, mine, owned], dst_ref=ref.at[part_of, mine, owned],
                send_sem=gather_send.at[which, step], recv_sem=gather_recv.at[which, step],
                device_id=(own * half + lax.rem(x + step, half), gy, gz), device_id_type=MESH).wait_recv()
        for step in range(1, half):
            gather_copy(which, ref, base, step).wait_send()

    def cross_copies(stage, ref, base, number):
        tiles = pl.ds(0, max(1, number // 8))
        body = slice(base, base + number)

        def to(index, source, target, device):
            return pltpu.make_async_remote_copy(
                src_ref=source, dst_ref=target, send_sem=cross_send.at[stage, index],
                recv_sem=cross_recv.at[stage, index], device_id=device, device_id_type=MESH)

        def pack(index, side, block, device):
            return to(index, zs.at[stage, side, tiles], zr.at[stage, side, block, tiles], device)

        block = ref.at[body, mine, owned]
        sent = (
            (has_y_up, to(0, block, ref.at[body, 16:24, owned], y_up)),
            (has_y_down, to(1, block, ref.at[body, 8:16, owned], y_down)),
            (has_z_up, pack(2, 0, 0, z_up)),
            (has_z_down, pack(3, 1, 0, z_down)),
            (corners[0][0], pack(4, 0, 2, corners[0][1])),
            (corners[1][0], pack(5, 1, 2, corners[1][1])),
            (corners[2][0], pack(6, 0, 1, corners[2][1])),
            (corners[3][0], pack(7, 1, 1, corners[3][1])),
        )
        opposite = (has_y_down, has_y_up, has_z_down, has_z_up,
                    corners[3][0], corners[2][0], corners[1][0], corners[0][0])
        arrive = tuple((there, sent[i][1]) for i, there in enumerate(opposite))
        return sent, arrive

    def cross_start(stage, ref, base, number):
        for t in range(max(1, number // 8)):
            high, low = jnp.zeros((8, 128), jnp.float32), jnp.zeros((8, 128), jnp.float32)
            for i in range(min(8, number)):
                value = ref[base + 8 * t + i, mine, owned]
                here = (lane8 >= 16 * i) & (lane8 < 16 * i + 16)
                high = jnp.where(here, pltpu.roll(value, (16 * i + 16) % 128, 1), high)
                low = jnp.where(here, pltpu.roll(value, 16 * i, 1), low)
            zs[stage, 0, t] = high
            zs[stage, 1, t] = low
        each(cross_copies(stage, ref, base, number)[0], lambda copy: copy.start())

    def cross_finish(stage, ref, base, number):
        sent, arrive = cross_copies(stage, ref, base, number)
        each(arrive, lambda copy: copy.wait_recv())
        each(sent, lambda copy: copy.wait_send())
        for t in range(max(1, number // 8)):
            for block in range(3):
                below, above = zr[stage, 0, block, t], zr[stage, 1, block, t]
                for i in range(min(8, number)):
                    ref[base + 8 * t + i, 8 * block : 8 * block + 8, 128:256] = jnp.where(
                        lane8 < 16, pltpu.roll(above, (128 - 16 * i) % 128, 1),
                        jnp.where(lane8 >= 112, pltpu.roll(below, (112 - 16 * i) % 128, 1), 0.0))

    def edges(ref, number):
        ref[0] = jnp.where(odd, pltpu.roll(ref[number], 1, 1), 0.0)
        ref[number + 1] = jnp.where(odd, 0.0, pltpu.roll(ref[1], 255, 1))

    GROUP = 2

    def groups(number):
        return [(a, a + GROUP) for a in range(0, number, GROUP)]

    def spread(ref, a, b, level):
        w = level
        value = ref[1 + a : 1 + b]
        return value, (
            ref[a:b], ref[a + 2 : b + 2],
            pltpu.roll(value, w, 1), pltpu.roll(value, 24 - w, 1),
            pltpu.roll(value, 2 * w, 2), pltpu.roll(value, 256 - 2 * w, 2),
        )

    def coarse_faces(level, ref, number, gref, dref):
        edges(ref, number)
        for a, b in groups(number):
            value, around = spread(ref, a, b, level)
            faces = [0.5 * (value + other) for other in around]
            diagonal = faces[0]
            for face in faces[1:]:
                diagonal = diagonal + face
            inverse = jnp.where(value > 0.0, 1.0 / diagonal, 0.0)
            for i in range(6):
                gref[i, a:b] = faces[i] * inverse
            dref[0, a:b] = diagonal * 0.25**level
            dref[1, a:b] = inverse * 4.0**level

    def coarse_total(level, ref, a, b, right, gref):
        value, around = spread(ref, a, b, level)
        total = right[a:b] - value
        for i in range(6):
            total = total + gref[i, a:b] * around[i]
        return value, total

    def coarse_smooth(level, begin, buffers, number, right, gref, uref):
        rho = 1.0 / SIGMA
        now, sweeps = begin, []
        if begin is None:
            now, buffers = buffers[0], buffers[1:] + buffers[:1]
            for a, b in groups(number):
                u = right[a:b] * (1.0 / CENTRE)
                uref[a:b] = u
                now[1 + a : 1 + b] = u
        else:
            sweeps = [(0.0, 1.0 / CENTRE)]
        for _ in range(DEGREE - 1):
            rho_next = 1.0 / (2.0 * SIGMA - rho)
            sweeps.append((rho_next * rho, 2.0 * rho_next / HALF))
            rho = rho_next
        for old, new in sweeps:
            then, buffers = buffers[0], buffers[1:] + buffers[:1]
            edges(now, number)
            for a, b in groups(number):
                value, total = coarse_total(level, now, a, b, right, gref)
                u = new * total
                if old:
                    u = old * uref[a:b] + u
                uref[a:b] = u
                then[1 + a : 1 + b] = value + u
            now = then
        return now

    def coarse_restrict(pairs):
        value = pairs[0] + pairs[1]
        value = value + jnp.where(lax.rem(wide_row, 2) == 0, pltpu.roll(value, 23, 0), pltpu.roll(value, 1, 0))
        value = value + jnp.where(lax.rem(wide_lane, 4) < 2, pltpu.roll(value, 254, 1), pltpu.roll(value, 2, 1))
        return value * 0.125

    tall_row, tall_lane = (lax.broadcasted_iota(jnp.int32, (32, 256), d) for d in range(2))
    tall_odd = lax.rem(tall_lane, 2)
    strip = lax.broadcasted_iota(jnp.int32, (32, 128), 1)
    inner = x < half - 1
    outer = x > 0

    def side_copies(which, ref, near, far):
        def to(index, arrival, source, target, device):
            return pltpu.make_async_remote_copy(
                src_ref=source, dst_ref=ref.at[target, 0:16, owned], send_sem=side_send.at[which, index],
                recv_sem=side_recv.at[which, arrival], device_id=device, device_id_type=MESH)

        low, high = slice(0, 5), slice(13, 18)
        sent = (
            (inner, to(0, 0, near.at[3:8], low, x_right)),
            ((x == half - 1) & (own == 1), to(1, 0, far.at[3:8], low, x_right)),
            (outer, to(2, 1, near.at[0:5], high, x_left)),
            ((x == 0) & (own == 0), to(3, 1, far.at[0:5], high, x_left)),
        )
        arrive = ((outer | (own == 1), to(0, 0, near.at[3:8], low, x_right)),
                  (inner | (own == 0), to(2, 1, near.at[0:5], high, x_left)))
        return sent, arrive

    def side_start(which, ref, near, far):
        ref[5:13, 0:16, owned] = near[...]
        each(side_copies(which, ref, near, far)[0], lambda copy: copy.start())

    def side_finish(which, ref, near, far):
        sent, arrive = side_copies(which, ref, near, far)
        each(arrive, lambda copy: copy.wait_recv())
        each(sent, lambda copy: copy.wait_send())

    def deep_copies(which, ref):
        def to(index, source, target, device):
            return pltpu.make_async_remote_copy(
                src_ref=source, dst_ref=target, send_sem=deep_send.at[which, index],
                recv_sem=deep_recv.at[which, index], device_id=device, device_id_type=MESH)

        def pack(index, side, block, device):
            return to(index, ez.at[which, side], er.at[which, side, block], device)

        sent = (
            (has_y_up, to(0, ref.at[:, 8:16, owned], ref.at[:, 24:32, owned], y_up)),
            (has_y_down, to(1, ref.at[:, 0:8, owned], ref.at[:, 16:24, owned], y_down)),
            (has_z_up, pack(2, 0, 0, z_up)),
            (has_z_down, pack(3, 1, 0, z_down)),
            (corners[0][0], pack(4, 0, 2, corners[0][1])),
            (corners[1][0], pack(5, 1, 2, corners[1][1])),
            (corners[2][0], pack(6, 0, 1, corners[2][1])),
            (corners[3][0], pack(7, 1, 1, corners[3][1])),
        )
        opposite = (has_y_down, has_y_up, has_z_down, has_z_up,
                    corners[3][0], corners[2][0], corners[1][0], corners[0][0])
        return sent, tuple((there, sent[i][1]) for i, there in enumerate(opposite))

    def deep_start(which, ref):
        high, low = jnp.zeros((16, 128), jnp.float32), jnp.zeros((16, 128), jnp.float32)
        for i in range(18):
            value = ref[i, 0:16, owned]
            here = (lane >= 7 * i) & (lane < 7 * i + 7)
            high = jnp.where(here, pltpu.roll(value, (7 * i + 7) % 128, 1), high)
            low = jnp.where(here, pltpu.roll(value, 7 * i, 1), low)
        ez[which, 0] = high
        ez[which, 1] = low
        each(deep_copies(which, ref)[0], lambda copy: copy.start())

    def deep_finish(which, ref):
        sent, arrive = deep_copies(which, ref)
        each(arrive, lambda copy: copy.wait_recv())
        each(sent, lambda copy: copy.wait_send())
        below, above = (
            jnp.concatenate([er[which, side, 0], er[which, side, 1, 0:8], er[which, side, 2, 8:16]]) for side in range(2))
        for i in range(18):
            ref[i, :, 128:256] = jnp.where(
                strip < 7, pltpu.roll(above, (128 - 7 * i) % 128, 1),
                jnp.where(strip >= 121, pltpu.roll(below, (121 - 7 * i) % 128, 1), 0.0))

    def deep_around(ref, a, b):
        value = ref[a:b]
        return value, (
            ref[a - 1 : b - 1], ref[a + 1 : b + 1], pltpu.roll(value, 1, 1), pltpu.roll(value, 31, 1),
            pltpu.roll(value, 1, 2), pltpu.roll(value, 255, 2),
        )

    def deep_faces():
        for i in range(1, 17):
            value, around = deep_around(ek, i, i + 1)
            faces = [0.5 * (value + other) for other in around]
            diagonal = faces[0]
            for face in faces[1:]:
                diagonal = diagonal + face
            inverse = jnp.where(value > 0.0, 1.0 / diagonal, 0.0)
            for f in range(6):
                eg[f, i - 1 : i] = faces[f] * inverse
            eb[i : i + 1] = eb[i : i + 1] * inverse

    def deep_total(ref, a, b):
        value, around = deep_around(ref, a, b)
        total = eb[a:b] - value
        for f in range(6):
            total = total + eg[f, a - 1 : b - 1] * around[f]
        return value, total

    def deep_correct(coarse):
        for j in range(-3, 7):
            spot = 4 * x + j
            kind = own
            place = 1 + spot
            if j < 0:
                wrapped = spot < 0
                place = jnp.where(wrapped, place + count1, place)
                kind = jnp.where(wrapped, 0, own)
                there = jnp.logical_not(wrapped & (own == 0))
            elif j > 3:
                wrapped = spot >= count1
                place = jnp.where(wrapped, place - count1, place)
                kind = jnp.where(wrapped, 1, own)
                there = jnp.logical_not(wrapped & (own == 1))
            else:
                there = None
            value = coarse[place]
            value = jnp.where(lax.rem(wide_lane, 2) == kind, value,
                              jnp.where(odd, pltpu.roll(value, 1, 1), pltpu.roll(value, 255, 1)))
            if there is not None:
                value = jnp.where(there, value, 0.0)
            for shift in range(2):
                for c in range(2):
                    cols = slice(128 * c, 128 * c + 128)
                    spill[c, pl.ds(shift, 8, stride=2), :] = value[0:8, cols]
                    spill[c, pl.ds(16 + shift, 4, stride=2), :] = value[8:12, cols]
                    spill[c, pl.ds(24 + shift, 4, stride=2), :] = value[20:24, cols]
            for i in (2 * j + 5, 2 * j + 6):
                if 0 <= i < 18:
                    for c in range(2):
                        cols = slice(128 * c, 128 * c + 128)
                        exa[i, :, cols] = exa[i, :, cols] + spill[c]

    xs[0][0, own, 1:9] = coef_ref[...]
    xs[0][0, 1 - own, 1:9] = relay_k[...]
    start(0, 0)
    gather_start(0, k1, 1, [restrict(xs[0][0, s, 1:9], 1) for s in range(2)])
    finish(0, 0)
    for s in range(2):
        value, around = neighbours(0, 0, s)
        faces = [0.5 * (value + other) for other in around]
        diagonal = faces[0]
        for face in faces[1:]:
            diagonal = diagonal + face
        inverse = 1.0 / diagonal
        for i in range(6):
            gs[0][i, s] = faces[i] * inverse
        ds[0][0, s] = diagonal
        ds[0][1, s] = inverse
    swap(1).wait()
    bs[0][own] = right_ref[...]
    bs[0][1 - own] = relay_b[...]
    for s in range(2):
        bs[0][s] = bs[0][s] * ds[0][1, s]
    state["par"] = 1

    def between(sweep):
        if sweep == 0:
            gather_finish(0, k1, 1)
            cross_start(0, k1, 1, count1)
            side_start(0, ek, coef_ref, relay_k)
            side_start(1, eb, right_ref, relay_b)
        if sweep == 1:
            cross_finish(0, k1, 1, count1)
            side_finish(0, ek, coef_ref, relay_k)
            side_finish(1, eb, right_ref, relay_b)
            deep_start(0, ek)
            deep_start(1, eb)
            coarse_faces(1, k1, count1, g1, d1)
        if sweep == 2:
            for m in range(count2):
                k2[1 + m] = coarse_restrict(k1[1 + 2 * m : 3 + 2 * m])
            coarse_faces(2, k2, count2, g2, d2)
            deep_finish(0, ek)
            deep_finish(1, eb)

    smooth(0, True, between)
    held = state["par"]
    start(0, held)
    near, far = xs[0].at[held, own, 1:9], xs[0].at[held, 1 - own, 1:9]
    side_start(2, exa, near, far)
    finish(0, held)
    fine = []
    for s in range(2):
        _, total = scaled_residual(0, held, s)
        fine.append(restrict(total * ds[0][0, s], 1))
    gather_start(1, r1, 0, fine)
    side_finish(2, exa, near, far)
    deep_start(2, exa)
    gather_finish(1, r1, 0)
    cross_start(1, r1, 0, count1)
    deep_faces()
    cross_finish(1, r1, 0, count1)
    for a, b in groups(count1):
        r1[a:b] = r1[a:b] * d1[1, a:b]
    now = coarse_smooth(1, None, [x1a, x1b], count1, r1, g1, u1)
    edges(now, count1)
    for m in range(count2):
        _, total = coarse_total(1, now, 2 * m, 2 * m + 2, r1, g1)
        r2[m, mine, owned] = coarse_restrict(total * d1[0, 2 * m : 2 * m + 2])[mine, owned]
    cross_start(2, r2, 0, count2)
    cross_finish(2, r2, 0, count2)
    for a, b in groups(count2):
        r2[a:b] = r2[a:b] * d2[1, a:b]
    deep = coarse_smooth(2, None, [x2a, x2b], count2, r2, g2, u2)
    for q in range(count1):
        x1s[1 + q, mine, owned] = now[1 + q, mine, owned] + deep[1 + q // 2, mine, owned]
    cross_start(3, x1s, 1, count1)
    deep_finish(2, exa)
    cross_finish(3, x1s, 1, count1)
    now = coarse_smooth(1, x1s, [x1a, x1b], count1, r1, g1, u1)
    deep_correct(now)
    rho = 1.0 / SIGMA
    sweeps = [(0.0, 1.0 / CENTRE)]
    for _ in range(DEGREE - 1):
        rho_next = 1.0 / (2.0 * SIGMA - rho)
        sweeps.append((rho_next * rho, 2.0 * rho_next / HALF))
        rho = rho_next
    now, then = exa, exb
    for depth, (old, new) in enumerate(sweeps):
        for i in range(1 + depth, 17 - depth):
            value, total = deep_total(now, i, i + 1)
            u = new * total
            if old:
                u = old * eu[i - 1 : i] + u
            eu[i - 1 : i] = u
            then[i : i + 1] = value + u
        now, then = then, now
    for p in range(8):
        value, total = deep_total(now, 5 + p, 6 + p)
        sol_ref[p] = value[0, 0:16, owned]
        res_ref[p] = total[0, 0:16, owned] * ds[0][0, own, p]


def solution(mesh):
    sizes = tuple(mesh.shape[a] for a in ("gx", "gy", "gz"))
    vmem = pltpu.VMEM
    f32 = jnp.float32
    half = sizes[0] // 2
    n1, n2 = 4 * half, 2 * half
    dma = pltpu.SemaphoreType.DMA

    def big(*lead):
        return vmem((*lead, 24, 256), f32)

    scratch = [
        vmem((2, 2, 10, 16, 128), f32), vmem((6, 2, 8, 16, 128), f32), vmem((2, 8, 16, 128), f32),
        vmem((2, 8, 16, 128), f32), vmem((2, 2, 8, 16, 128), f32),
        *[vmem((1, 2, 2, 16, 128), f32)] * 4,
        *[vmem((8, 16, 128), f32)] * 2,
        *[dma((1, 2, 8))] * 2, *[dma((2,))] * 2,
        big(n1 + 2), big(n1), big(n1 + 2), big(n1 + 2), big(n1 + 2), big(6, n1), big(n1), big(2, n1),
        big(n2 + 2), big(n2), big(n2 + 2), big(n2 + 2), big(6, n2), big(n2), big(2, n2),
        vmem((2, 4, 16, 128), f32), vmem((4, 2, 2, 8, 128), f32), vmem((4, 2, 3, 2, 8, 128), f32),
        *[dma((2, half))] * 2, *[dma((4, 8))] * 2,
        *[vmem((18, 32, 256), f32)] * 4, vmem((6, 16, 32, 256), f32), vmem((16, 32, 256), f32),
        vmem((3, 2, 16, 128), f32), vmem((3, 2, 3, 16, 128), f32), *[dma((3, 4))] * 2, *[dma((3, 8))] * 2,
        vmem((2, 32, 128), f32),
    ]

    def per_device(right_side, coefficient):
        return pl.pallas_call(
            functools.partial(kernel, sizes),
            out_shape=(jax.ShapeDtypeStruct((8, 16, 128), f32),) * 2,
            in_specs=[pl.BlockSpec(memory_space=vmem)] * 2,
            out_specs=(pl.BlockSpec(memory_space=vmem),) * 2,
            scratch_shapes=scratch,
            compiler_params=pltpu.CompilerParams(collective_id=0, has_side_effects=True),
            name="vcycle",
        )(right_side, coefficient)

    specs = (P("gx", "gy", "gz"), P("gx", "gy", "gz"))
    return jax.shard_map(per_device, mesh=mesh, in_specs=specs, out_specs=specs, check_vma=False)
```

```python
import functools

import jax
import jax.numpy as jnp
from jax import lax
from jax.experimental import pallas as pl
from jax.experimental.pallas import tpu as pltpu
from jax.sharding import PartitionSpec as P

DEGREE = 4
cheb_low = 0.3
cheb_high = 2.0
CENTRE = 0.5 * (cheb_high + cheb_low)
HALF = 0.5 * (cheb_high - cheb_low)
SIGMA = CENTRE / HALF
MESH = pl.DeviceIdType.MESH


def kernel(sizes, right_ref, coef_ref, sol_ref, res_ref, *scratch):
    (x0, g0, u0, b0, d0, hy, sy, hz, sz, relay_b, relay_k, send_sem, recv_sem, relay_send, relay_recv,
     k1, r1, x1a, x1b, x1s, g1, u1, d1, k2, r2, x2a, x2b, g2, u2, d2, wide, zs, zr,
     gather_send, gather_recv, cross_send, cross_recv,
     ek, eb, exa, exb, eg, eu, ez, er, side_send, side_recv, deep_send, deep_recv, spill) = scratch
    xs, gs, us, bs, ds = (x0,), (g0,), (u0,), (b0,), (d0,)
    size_gx, size_gy, size_gz = sizes
    half = size_gx // 2
    gx, gy, gz = lax.axis_index("gx"), lax.axis_index("gy"), lax.axis_index("gz")
    own = gx // half
    x = gx % half

    across = ((1 - own) * half + x, gy, gz)

    x_right = (own * half + lax.rem(x + 1, half), gy, gz)
    x_left = (own * half + lax.rem(x + half - 1, half), gy, gz)
    y_up, y_down = (gx, gy + 1, gz), (gx, gy - 1, gz)
    z_up, z_down = (gx, gy, gz + 1), (gx, gy, gz - 1)
    has_y_up, has_y_down = gy < size_gy - 1, gy > 0
    has_z_up, has_z_down = gz < size_gz - 1, gz > 0
    optional = ((has_y_up, y_up), (has_y_down, y_down), (has_z_up, z_up), (has_z_down, z_down))

    def zero(ref):
        ref[...] = jnp.zeros_like(ref)

    for ref in (*xs, hy, sy, hz, sz, k1, r1, x1s, r2, zs, zr, ek, eb, exa, er):
        zero(ref)

    barrier = pltpu.get_barrier_semaphore()
    for device in (x_right, x_left, across):
        pl.semaphore_signal(barrier, inc=1, device_id=device, device_id_type=MESH)
    corners = (
        (has_y_up & has_z_up, (gx, gy + 1, gz + 1)),
        (has_y_up & has_z_down, (gx, gy + 1, gz - 1)),
        (has_y_down & has_z_up, (gx, gy - 1, gz + 1)),
        (has_y_down & has_z_down, (gx, gy - 1, gz - 1)),
    )
    for there, device in (*optional, *corners):
        @pl.when(there)
        def _():
            pl.semaphore_signal(barrier, inc=1, device_id=device, device_id_type=MESH)
    count = 1 + max(half - 1, 2)
    for step in range(2, half - 1):
        device = (own * half + lax.rem(x + step, half), gy, gz)
        pl.semaphore_signal(barrier, inc=1, device_id=device, device_id_type=MESH)
    for there, _ in (*optional, *corners):
        count = count + there.astype(jnp.int32)
    pl.semaphore_wait(barrier, count)

    def swap(which):
        source, target = ((coef_ref, relay_k), (right_ref, relay_b))[which]
        return pltpu.make_async_remote_copy(
            src_ref=source, dst_ref=target, send_sem=relay_send.at[which], recv_sem=relay_recv.at[which],
            device_id=across, device_id_type=MESH)

    swap(0).start()
    swap(0).wait_send()
    swap(1).start()
    swap(0).wait_recv()

    row = lax.broadcasted_iota(jnp.int32, (16, 128), 0)
    lane = lax.broadcasted_iota(jnp.int32, (16, 128), 1)

    def remote(level, par, index, source, target, device):
        return pltpu.make_async_remote_copy(
            src_ref=source, dst_ref=target, send_sem=send_sem.at[level, par, index[0]],
            recv_sem=recv_sem.at[level, par, index[1]], device_id=device, device_id_type=MESH)

    def planes(level):
        return xs[level].shape[2] - 2

    def copies(level, par):
        n = planes(level)
        buf = xs[level]
        over = (x == half - 1).astype(jnp.int32)
        under = (x > 0).astype(jnp.int32)
        used = max(8, 2 * n)
        rows = pl.ds(0, used)
        right = (
            (None, remote(level, par, (0, over), buf.at[par, 0, n], buf.at[par, over, 0], x_right)),
            (x < half - 1, remote(level, par, (1, 1), buf.at[par, 1, n], buf.at[par, 1, 0], x_right)),
            (None, remote(level, par, (2, 2 + under), buf.at[par, 1, 1], buf.at[par, under, n + 1], x_left)),
            (x > 0, remote(level, par, (3, 2), buf.at[par, 0, 1], buf.at[par, 0, n + 1], x_left)),
            (has_y_up, remote(level, par, (4, 4), sy.at[level, par, 0, rows], hy.at[level, par, 0, rows], y_up)),
            (has_y_down, remote(level, par, (5, 5), sy.at[level, par, 1, rows], hy.at[level, par, 1, rows], y_down)),
            (has_z_up, remote(level, par, (6, 6), sz.at[level, par, 0], hz.at[level, par, 0], z_up)),
            (has_z_down, remote(level, par, (7, 7), sz.at[level, par, 1], hz.at[level, par, 1], z_down)),
        )
        arrive = (
            (x > 0, remote(level, par, (0, 0), buf.at[par, 0, n], buf.at[par, 0, 0], x_right)),
            (None, remote(level, par, (1, 1), buf.at[par, 1, n], buf.at[par, 1, 0], x_right)),
            (None, remote(level, par, (3, 2), buf.at[par, 0, 1], buf.at[par, 0, n + 1], x_left)),
            (x < half - 1, remote(level, par, (2, 3), buf.at[par, 1, 1], buf.at[par, 1, n + 1], x_left)),
            (has_y_down, right[4][1]),
            (has_y_up, right[5][1]),
            (has_z_down, right[6][1]),
            (has_z_up, right[7][1]),
        )
        return right, arrive

    def each(listed, act):
        for there, copy in listed:
            if there is None:
                act(copy)
            else:
                @pl.when(there)
                def _():
                    act(copy)

    def start(level, par):
        n, w = planes(level), 2**level
        buf = xs[level]
        to_up, to_down = jnp.zeros((16, 128), jnp.float32), jnp.zeros((16, 128), jnp.float32)
        for s in range(2):
            sy[level, par, 0, s * n : (s + 1) * n, :] = buf[par, s, 1 : n + 1, 15, :]
            sy[level, par, 1, s * n : (s + 1) * n, :] = buf[par, s, 1 : n + 1, 0, :]
            for p in range(n):
                at = (s * n + p) * w
                here = (lane >= at) & (lane < at + w)
                value = buf[par, s, 1 + p]
                to_up = jnp.where(here, pltpu.roll(value, (at + w) % 128, 1), to_up)
                to_down = jnp.where(here, pltpu.roll(value, at, 1), to_down)
        sz[level, par, 0] = to_up
        sz[level, par, 1] = to_down
        each(copies(level, par)[0], lambda copy: copy.start())

    def finish(level, par):
        sent, arrive = copies(level, par)
        each(arrive, lambda copy: copy.wait_recv())
        each(sent, lambda copy: copy.wait_send())

    def neighbours(level, par, s):
        n, w = planes(level), 2**level
        buf = xs[level]
        value = buf[par, s, 1 : n + 1]
        low, high = hz[level, par, 0], hz[level, par, 1]
        shape = (n, 16, 128)
        lows = jnp.stack([pltpu.roll(low, (128 - (s * n + p) * w) % 128, 1) for p in range(n)])
        highs = jnp.stack([pltpu.roll(high, (128 - w - (s * n + p) * w) % 128, 1) for p in range(n)])
        under = jnp.broadcast_to(hy[level, par, 0, s * n : (s + 1) * n, :][:, None, :], shape)
        over = jnp.broadcast_to(hy[level, par, 1, s * n : (s + 1) * n, :][:, None, :], shape)
        return value, (
            buf[par, s, 0:n],
            buf[par, s, 2 : n + 2],
            jnp.where(row < w, under, pltpu.roll(value, w, 1)),
            jnp.where(row >= 16 - w, over, pltpu.roll(value, 16 - w, 1)),
            jnp.where(lane < w, lows, pltpu.roll(value, w, 2)),
            jnp.where(lane >= 128 - w, highs, pltpu.roll(value, 128 - w, 2)),
        )

    def scaled_residual(level, par, s):
        value, around = neighbours(level, par, s)
        total = bs[level][s] - value
        for i in range(6):
            total = total + gs[level][i, s] * around[i]
        return value, total

    def inside(level):
        return slice(1, planes(level) + 1)

    state = {"par": 0}

    def smooth(level, fresh, between=None):
        keep = inside(level)
        rho = 1.0 / SIGMA
        par = state["par"]
        if fresh:
            for s in range(2):
                u = bs[level][s] * (1.0 / CENTRE)
                us[level][s] = u
                xs[level][par, s, keep] = u
        sweeps = [] if fresh else [(0.0, 1.0 / CENTRE)]
        for _ in range(DEGREE - 1):
            rho_next = 1.0 / (2.0 * SIGMA - rho)
            sweeps.append((rho_next * rho, 2.0 * rho_next / HALF))
            rho = rho_next
        for number, (old, new) in enumerate(sweeps):
            start(level, par)
            if between:
                between(number)
            finish(level, par)
            for s in range(2):
                value, total = scaled_residual(level, par, s)
                u = new * total
                if old:
                    u = old * us[level][s] + u
                us[level][s] = u
                xs[level][1 - par, s, keep] = value + u
            par = 1 - par
        state["par"] = par

    def pair_sum(value, w):
        even_row = lax.rem(row, 2 * w) < w
        value = value + jnp.where(even_row, pltpu.roll(value, 16 - w, 1), pltpu.roll(value, w, 1))
        even_lane = lax.rem(lane, 2 * w) < w
        return value + jnp.where(even_lane, pltpu.roll(value, 128 - w, 2), pltpu.roll(value, w, 2))

    def restrict(value, w):
        total = pair_sum(value, w)
        return jnp.stack([total[2 * p] + total[2 * p + 1] for p in range(value.shape[0] // 2)]) * 0.125

    count1, count2 = 4 * half, 2 * half
    wide_row = lax.broadcasted_iota(jnp.int32, (24, 256), 0)
    wide_lane = lax.broadcasted_iota(jnp.int32, (24, 256), 1)
    odd = lax.rem(wide_lane, 2) == 1
    lane8 = lax.broadcasted_iota(jnp.int32, (8, 128), 1)
    odd8 = lax.rem(lane8, 2) == 1
    mine, owned = slice(0, 8), slice(0, 128)

    def gather_copy(which, ref, base, step):
        part_of = pl.ds(base + 4 * x, 4)
        return pltpu.make_async_remote_copy(
            src_ref=ref.at[part_of, mine, owned], dst_ref=ref.at[part_of, mine, owned],
            send_sem=gather_send.at[which, step], recv_sem=gather_recv.at[which, step],
            device_id=(own * half + lax.rem(x + step, half), gy, gz), device_id_type=MESH)

    def gather_start(which, ref, base, values):
        for s in range(2):
            wide[s] = values[s]
        for p in range(4):
            low, high = wide[0, p, pl.ds(0, 8, stride=2), :], wide[1, p, pl.ds(0, 8, stride=2), :]
            ref[base + 4 * x + p, mine, owned] = jnp.where(odd8, high, low)
        for step in range(1, half):
            gather_copy(which, ref, base, step).start()

    def gather_finish(which, ref, base):
        for step in range(1, half):
            source = lax.rem(x + half - step, half)
            part_of = pl.ds(base + 4 * source, 4)
            pltpu.make_async_remote_copy(
                src_ref=ref.at[part_of, mine, owned], dst_ref=ref.at[part_of, mine, owned],
                send_sem=gather_send.at[which, step], recv_sem=gather_recv.at[which, step],
                device_id=(own * half + lax.rem(x + step, half), gy, gz), device_id_type=MESH).wait_recv()
        for step in range(1, half):
            gather_copy(which, ref, base, step).wait_send()

    def cross_copies(stage, ref, base, number):
        tiles = pl.ds(0, max(1, number // 8))
        body = slice(base, base + number)

        def to(index, source, target, device):
            return pltpu.make_async_remote_copy(
                src_ref=source, dst_ref=target, send_sem=cross_send.at[stage, index],
                recv_sem=cross_recv.at[stage, index], device_id=device, device_id_type=MESH)

        def pack(index, side, block, device):
            return to(index, zs.at[stage, side, tiles], zr.at[stage, side, block, tiles], device)

        block = ref.at[body, mine, owned]
        sent = (
            (has_y_up, to(0, block, ref.at[body, 16:24, owned], y_up)),
            (has_y_down, to(1, block, ref.at[body, 8:16, owned], y_down)),
            (has_z_up, pack(2, 0, 0, z_up)),
            (has_z_down, pack(3, 1, 0, z_down)),
            (corners[0][0], pack(4, 0, 2, corners[0][1])),
            (corners[1][0], pack(5, 1, 2, corners[1][1])),
            (corners[2][0], pack(6, 0, 1, corners[2][1])),
            (corners[3][0], pack(7, 1, 1, corners[3][1])),
        )
        opposite = (has_y_down, has_y_up, has_z_down, has_z_up,
                    corners[3][0], corners[2][0], corners[1][0], corners[0][0])
        arrive = tuple((there, sent[i][1]) for i, there in enumerate(opposite))
        return sent, arrive

    def cross_start(stage, ref, base, number):
        for t in range(max(1, number // 8)):
            high, low = jnp.zeros((8, 128), jnp.float32), jnp.zeros((8, 128), jnp.float32)
            for i in range(min(8, number)):
                value = ref[base + 8 * t + i, mine, owned]
                here = (lane8 >= 16 * i) & (lane8 < 16 * i + 16)
                high = jnp.where(here, pltpu.roll(value, (16 * i + 16) % 128, 1), high)
                low = jnp.where(here, pltpu.roll(value, 16 * i, 1), low)
            zs[stage, 0, t] = high
            zs[stage, 1, t] = low
        each(cross_copies(stage, ref, base, number)[0], lambda copy: copy.start())

    def cross_finish(stage, ref, base, number):
        sent, arrive = cross_copies(stage, ref, base, number)
        each(arrive, lambda copy: copy.wait_recv())
        each(sent, lambda copy: copy.wait_send())
        for t in range(max(1, number // 8)):
            for block in range(3):
                below, above = zr[stage, 0, block, t], zr[stage, 1, block, t]
                for i in range(min(8, number)):
                    ref[base + 8 * t + i, 8 * block : 8 * block + 8, 128:256] = jnp.where(
                        lane8 < 16, pltpu.roll(above, (128 - 16 * i) % 128, 1),
                        jnp.where(lane8 >= 112, pltpu.roll(below, (112 - 16 * i) % 128, 1), 0.0))

    def edges(ref, number):
        ref[0] = jnp.where(odd, pltpu.roll(ref[number], 1, 1), 0.0)
        ref[number + 1] = jnp.where(odd, 0.0, pltpu.roll(ref[1], 255, 1))

    GROUP = 2

    def groups(number):
        return [(a, a + GROUP) for a in range(0, number, GROUP)]

    def spread(ref, a, b, level):
        w = level
        value = ref[1 + a : 1 + b]
        return value, (
            ref[a:b], ref[a + 2 : b + 2],
            pltpu.roll(value, w, 1), pltpu.roll(value, 24 - w, 1),
            pltpu.roll(value, 2 * w, 2), pltpu.roll(value, 256 - 2 * w, 2),
        )

    def coarse_faces(level, ref, number, gref, dref):
        edges(ref, number)
        for a, b in groups(number):
            value, around = spread(ref, a, b, level)
            faces = [0.5 * (value + other) for other in around]
            diagonal = faces[0]
            for face in faces[1:]:
                diagonal = diagonal + face
            inverse = jnp.where(value > 0.0, 1.0 / diagonal, 0.0)
            for i in range(6):
                gref[i, a:b] = faces[i] * inverse
            dref[0, a:b] = diagonal * 0.25**level
            dref[1, a:b] = inverse * 4.0**level

    def coarse_total(level, ref, a, b, right, gref):
        value, around = spread(ref, a, b, level)
        total = right[a:b] - value
        for i in range(6):
            total = total + gref[i, a:b] * around[i]
        return value, total

    def coarse_smooth(level, begin, buffers, number, right, gref, uref):
        rho = 1.0 / SIGMA
        now, sweeps = begin, []
        if begin is None:
            now, buffers = buffers[0], buffers[1:] + buffers[:1]
            for a, b in groups(number):
                u = right[a:b] * (1.0 / CENTRE)
                uref[a:b] = u
                now[1 + a : 1 + b] = u
        else:
            sweeps = [(0.0, 1.0 / CENTRE)]
        for _ in range(DEGREE - 1):
            rho_next = 1.0 / (2.0 * SIGMA - rho)
            sweeps.append((rho_next * rho, 2.0 * rho_next / HALF))
            rho = rho_next
        for old, new in sweeps:
            then, buffers = buffers[0], buffers[1:] + buffers[:1]
            edges(now, number)
            for a, b in groups(number):
                value, total = coarse_total(level, now, a, b, right, gref)
                u = new * total
                if old:
                    u = old * uref[a:b] + u
                uref[a:b] = u
                then[1 + a : 1 + b] = value + u
            now = then
        return now

    def coarse_restrict(pairs):
        value = pairs[0] + pairs[1]
        value = value + jnp.where(lax.rem(wide_row, 2) == 0, pltpu.roll(value, 23, 0), pltpu.roll(value, 1, 0))
        value = value + jnp.where(lax.rem(wide_lane, 4) < 2, pltpu.roll(value, 254, 1), pltpu.roll(value, 2, 1))
        return value * 0.125

    tall_row, tall_lane = (lax.broadcasted_iota(jnp.int32, (32, 256), d) for d in range(2))
    tall_odd = lax.rem(tall_lane, 2)
    strip = lax.broadcasted_iota(jnp.int32, (32, 128), 1)
    inner = x < half - 1
    outer = x > 0

    def side_copies(which, ref, near, far):
        def to(index, arrival, source, target, device):
            return pltpu.make_async_remote_copy(
                src_ref=source, dst_ref=ref.at[target, 0:16, owned], send_sem=side_send.at[which, index],
                recv_sem=side_recv.at[which, arrival], device_id=device, device_id_type=MESH)

        low, high = slice(0, 5), slice(13, 18)
        sent = (
            (inner, to(0, 0, near.at[3:8], low, x_right)),
            ((x == half - 1) & (own == 1), to(1, 0, far.at[3:8], low, x_right)),
            (outer, to(2, 1, near.at[0:5], high, x_left)),
            ((x == 0) & (own == 0), to(3, 1, far.at[0:5], high, x_left)),
        )
        arrive = ((outer | (own == 1), to(0, 0, near.at[3:8], low, x_right)),
                  (inner | (own == 0), to(2, 1, near.at[0:5], high, x_left)))
        return sent, arrive

    def side_start(which, ref, near, far):
        ref[5:13, 0:16, owned] = near[...]
        each(side_copies(which, ref, near, far)[0], lambda copy: copy.start())

    def side_finish(which, ref, near, far):
        sent, arrive = side_copies(which, ref, near, far)
        each(arrive, lambda copy: copy.wait_recv())
        each(sent, lambda copy: copy.wait_send())

    def deep_copies(which, ref):
        def to(index, source, target, device):
            return pltpu.make_async_remote_copy(
                src_ref=source, dst_ref=target, send_sem=deep_send.at[which, index],
                recv_sem=deep_recv.at[which, index], device_id=device, device_id_type=MESH)

        def pack(index, side, block, device):
            return to(index, ez.at[which, side], er.at[which, side, block], device)

        sent = (
            (has_y_up, to(0, ref.at[:, 8:16, owned], ref.at[:, 24:32, owned], y_up)),
            (has_y_down, to(1, ref.at[:, 0:8, owned], ref.at[:, 16:24, owned], y_down)),
            (has_z_up, pack(2, 0, 0, z_up)),
            (has_z_down, pack(3, 1, 0, z_down)),
            (corners[0][0], pack(4, 0, 2, corners[0][1])),
            (corners[1][0], pack(5, 1, 2, corners[1][1])),
            (corners[2][0], pack(6, 0, 1, corners[2][1])),
            (corners[3][0], pack(7, 1, 1, corners[3][1])),
        )
        opposite = (has_y_down, has_y_up, has_z_down, has_z_up,
                    corners[3][0], corners[2][0], corners[1][0], corners[0][0])
        return sent, tuple((there, sent[i][1]) for i, there in enumerate(opposite))

    def deep_start(which, ref):
        high, low = jnp.zeros((16, 128), jnp.float32), jnp.zeros((16, 128), jnp.float32)
        for i in range(18):
            value = ref[i, 0:16, owned]
            here = (lane >= 7 * i) & (lane < 7 * i + 7)
            high = jnp.where(here, pltpu.roll(value, (7 * i + 7) % 128, 1), high)
            low = jnp.where(here, pltpu.roll(value, 7 * i, 1), low)
        ez[which, 0] = high
        ez[which, 1] = low
        each(deep_copies(which, ref)[0], lambda copy: copy.start())

    def deep_finish(which, ref):
        sent, arrive = deep_copies(which, ref)
        each(arrive, lambda copy: copy.wait_recv())
        each(sent, lambda copy: copy.wait_send())
        below, above = (
            jnp.concatenate([er[which, side, 0], er[which, side, 1, 0:8], er[which, side, 2, 8:16]]) for side in range(2))
        for i in range(18):
            ref[i, :, 128:256] = jnp.where(
                strip < 7, pltpu.roll(above, (128 - 7 * i) % 128, 1),
                jnp.where(strip >= 121, pltpu.roll(below, (121 - 7 * i) % 128, 1), 0.0))

    def deep_around(ref, a, b):
        value = ref[a:b]
        return value, (
            ref[a - 1 : b - 1], ref[a + 1 : b + 1], pltpu.roll(value, 1, 1), pltpu.roll(value, 31, 1),
            pltpu.roll(value, 1, 2), pltpu.roll(value, 255, 2),
        )

    def deep_faces():
        for i in range(1, 17):
            value, around = deep_around(ek, i, i + 1)
            faces = [0.5 * (value + other) for other in around]
            diagonal = faces[0]
            for face in faces[1:]:
                diagonal = diagonal + face
            inverse = jnp.where(value > 0.0, 1.0 / diagonal, 0.0)
            for f in range(6):
                eg[f, i - 1 : i] = faces[f] * inverse
            eb[i : i + 1] = eb[i : i + 1] * inverse

    def deep_total(ref, a, b):
        value, around = deep_around(ref, a, b)
        total = eb[a:b] - value
        for f in range(6):
            total = total + eg[f, a - 1 : b - 1] * around[f]
        return value, total

    def deep_correct(coarse):
        for j in range(-3, 7):
            spot = 4 * x + j
            kind = own
            place = 1 + spot
            if j < 0:
                wrapped = spot < 0
                place = jnp.where(wrapped, place + count1, place)
                kind = jnp.where(wrapped, 0, own)
                there = jnp.logical_not(wrapped & (own == 0))
            elif j > 3:
                wrapped = spot >= count1
                place = jnp.where(wrapped, place - count1, place)
                kind = jnp.where(wrapped, 1, own)
                there = jnp.logical_not(wrapped & (own == 1))
            else:
                there = None
            value = coarse[place]
            value = jnp.where(lax.rem(wide_lane, 2) == kind, value,
                              jnp.where(odd, pltpu.roll(value, 1, 1), pltpu.roll(value, 255, 1)))
            if there is not None:
                value = jnp.where(there, value, 0.0)
            for shift in range(2):
                for c in range(2):
                    cols = slice(128 * c, 128 * c + 128)
                    spill[c, pl.ds(shift, 8, stride=2), :] = value[0:8, cols]
                    spill[c, pl.ds(16 + shift, 4, stride=2), :] = value[8:12, cols]
                    spill[c, pl.ds(24 + shift, 4, stride=2), :] = value[20:24, cols]
            for i in (2 * j + 5, 2 * j + 6):
                if 0 <= i < 18:
                    for c in range(2):
                        cols = slice(128 * c, 128 * c + 128)
                        exa[i, :, cols] = exa[i, :, cols] + spill[c]

    xs[0][0, own, 1:9] = coef_ref[...]
    xs[0][0, 1 - own, 1:9] = relay_k[...]
    start(0, 0)
    gather_start(0, k1, 1, [restrict(xs[0][0, s, 1:9], 1) for s in range(2)])
    finish(0, 0)
    for s in range(2):
        value, around = neighbours(0, 0, s)
        faces = [0.5 * (value + other) for other in around]
        diagonal = faces[0]
        for face in faces[1:]:
            diagonal = diagonal + face
        inverse = 1.0 / diagonal
        for i in range(6):
            gs[0][i, s] = faces[i] * inverse
        ds[0][0, s] = diagonal
        ds[0][1, s] = inverse
    swap(1).wait()
    bs[0][own] = right_ref[...]
    bs[0][1 - own] = relay_b[...]
    for s in range(2):
        bs[0][s] = bs[0][s] * ds[0][1, s]
    state["par"] = 1

    def between(sweep):
        if sweep == 0:
            gather_finish(0, k1, 1)
            cross_start(0, k1, 1, count1)
            side_start(0, ek, coef_ref, relay_k)
            side_start(1, eb, right_ref, relay_b)
        if sweep == 1:
            cross_finish(0, k1, 1, count1)
            side_finish(0, ek, coef_ref, relay_k)
            side_finish(1, eb, right_ref, relay_b)
            coarse_faces(1, k1, count1, g1, d1)
        if sweep == 2:
            for m in range(count2):
                k2[1 + m] = coarse_restrict(k1[1 + 2 * m : 3 + 2 * m])
            coarse_faces(2, k2, count2, g2, d2)

    smooth(0, True, between)
    held = state["par"]
    start(0, held)
    near, far = xs[0].at[held, own, 1:9], xs[0].at[held, 1 - own, 1:9]
    side_start(2, exa, near, far)
    finish(0, held)
    fine = []
    for s in range(2):
        _, total = scaled_residual(0, held, s)
        fine.append(restrict(total * ds[0][0, s], 1))
    gather_start(1, r1, 0, fine)
    side_finish(2, exa, near, far)
    deep_start(2, exa)
    gather_finish(1, r1, 0)
    cross_start(1, r1, 0, count1)
    cross_finish(1, r1, 0, count1)
    for a, b in groups(count1):
        r1[a:b] = r1[a:b] * d1[1, a:b]
    now = coarse_smooth(1, None, [x1a, x1b], count1, r1, g1, u1)
    edges(now, count1)
    for m in range(count2):
        _, total = coarse_total(1, now, 2 * m, 2 * m + 2, r1, g1)
        r2[m, mine, owned] = coarse_restrict(total * d1[0, 2 * m : 2 * m + 2])[mine, owned]
    cross_start(2, r2, 0, count2)
    deep_start(0, ek)
    deep_start(1, eb)
    cross_finish(2, r2, 0, count2)
    for a, b in groups(count2):
        r2[a:b] = r2[a:b] * d2[1, a:b]
    deep = coarse_smooth(2, None, [x2a, x2b], count2, r2, g2, u2)
    for q in range(count1):
        x1s[1 + q, mine, owned] = now[1 + q, mine, owned] + deep[1 + q // 2, mine, owned]
    cross_start(3, x1s, 1, count1)
    deep_finish(2, exa)
    deep_finish(0, ek)
    deep_finish(1, eb)
    deep_faces()
    cross_finish(3, x1s, 1, count1)
    now = coarse_smooth(1, x1s, [x1a, x1b], count1, r1, g1, u1)
    deep_correct(now)
    rho = 1.0 / SIGMA
    sweeps = [(0.0, 1.0 / CENTRE)]
    for _ in range(DEGREE - 1):
        rho_next = 1.0 / (2.0 * SIGMA - rho)
        sweeps.append((rho_next * rho, 2.0 * rho_next / HALF))
        rho = rho_next
    now, then = exa, exb
    for depth, (old, new) in enumerate(sweeps):
        for i in range(1 + depth, 17 - depth):
            value, total = deep_total(now, i, i + 1)
            u = new * total
            if old:
                u = old * eu[i - 1 : i] + u
            eu[i - 1 : i] = u
            then[i : i + 1] = value + u
        now, then = then, now
    for p in range(8):
        value, total = deep_total(now, 5 + p, 6 + p)
        sol_ref[p] = value[0, 0:16, owned]
        res_ref[p] = total[0, 0:16, owned] * ds[0][0, own, p]


def solution(mesh):
    sizes = tuple(mesh.shape[a] for a in ("gx", "gy", "gz"))
    vmem = pltpu.VMEM
    f32 = jnp.float32
    half = sizes[0] // 2
    n1, n2 = 4 * half, 2 * half
    dma = pltpu.SemaphoreType.DMA

    def big(*lead):
        return vmem((*lead, 24, 256), f32)

    scratch = [
        vmem((2, 2, 10, 16, 128), f32), vmem((6, 2, 8, 16, 128), f32), vmem((2, 8, 16, 128), f32),
        vmem((2, 8, 16, 128), f32), vmem((2, 2, 8, 16, 128), f32),
        *[vmem((1, 2, 2, 16, 128), f32)] * 4,
        *[vmem((8, 16, 128), f32)] * 2,
        *[dma((1, 2, 8))] * 2, *[dma((2,))] * 2,
        big(n1 + 2), big(n1), big(n1 + 2), big(n1 + 2), big(n1 + 2), big(6, n1), big(n1), big(2, n1),
        big(n2 + 2), big(n2), big(n2 + 2), big(n2 + 2), big(6, n2), big(n2), big(2, n2),
        vmem((2, 4, 16, 128), f32), vmem((4, 2, 2, 8, 128), f32), vmem((4, 2, 3, 2, 8, 128), f32),
        *[dma((2, half))] * 2, *[dma((4, 8))] * 2,
        *[vmem((18, 32, 256), f32)] * 4, vmem((6, 16, 32, 256), f32), vmem((16, 32, 256), f32),
        vmem((3, 2, 16, 128), f32), vmem((3, 2, 3, 16, 128), f32), *[dma((3, 4))] * 2, *[dma((3, 8))] * 2,
        vmem((2, 32, 128), f32),
    ]

    def per_device(right_side, coefficient):
        found = pl.pallas_call(
            functools.partial(kernel, sizes),
            out_shape=(jax.ShapeDtypeStruct((8, 16, 128), f32),) * 2,
            in_specs=[pl.BlockSpec(memory_space=vmem)] * 2,
            out_specs=(pl.BlockSpec(memory_space=vmem),) * 2,
            scratch_shapes=scratch,
            compiler_params=pltpu.CompilerParams(collective_id=0, has_side_effects=True),
            name="vcycle",
        )(right_side, coefficient)

        def hand_on(a_ref, b_ref, c_ref, d_ref):
            c_ref[...] = a_ref[...]
            d_ref[...] = b_ref[...]

        return pl.pallas_call(
            hand_on,
            out_shape=(jax.ShapeDtypeStruct((8, 16, 128), f32),) * 2,
            in_specs=[pl.BlockSpec(memory_space=vmem)] * 2,
            out_specs=(pl.BlockSpec(memory_space=vmem),) * 2,
            name="hand_on",
        )(*found)

    specs = (P("gx", "gy", "gz"), P("gx", "gy", "gz"))
    return jax.shard_map(per_device, mesh=mesh, in_specs=specs, out_specs=specs, check_vma=False)
```
